32 devices in a mesh: dp: 16 (over z, y, x), tensor: 2 (over core).
Axes of the slice: x: 2, y: 2, z: 4, core: 2. Of those that a mesh axis runs over, the one named last changes fastest.
Arguments:
- text_input: bfloat16 [32, 512, 768], P(('dp', 'tensor')), may hold values from -6 to 6
- layout_input: bfloat16 [32, 512, 192], P(('dp', 'tensor')), may hold values from -6 to 6
- page_counts: int32 [32], P(('dp', 'tensor')), may hold values from 16 to 512, as said below
- text_joint: bfloat16 [768, 2304], replicated, may hold values from -0.21875 to 0.21875
- text_mixing: bfloat16 [768, 768], replicated, may hold values from -0.625 to 0.625
- text_norms: float32 [4, 768], replicated, may hold values from 0.1 to 1.9
- text_upward: bfloat16 [768, 3072], P(None, 'tensor'), may hold values from -0.21875 to 0.21875
- text_downward: bfloat16 [3072, 768], P('tensor'), may hold values from -0.109375 to 0.109375
- layout_joint: bfloat16 [192, 576], replicated, may hold values from -0.4375 to 0.4375
- layout_mixing: bfloat16 [192, 192], replicated, may hold values from -1.25 to 1.25
- layout_norms: float32 [4, 192], replicated, may hold values from 0.1 to 1.9
- layout_upward: bfloat16 [192, 768], P(None, 'tensor'), may hold values from -0.4375 to 0.4375
- layout_downward: bfloat16 [768, 192], P('tensor'), may hold values from -0.21875 to 0.21875
- text_cotangent: bfloat16 [32, 512, 768], P(('dp', 'tensor')), may hold values from -6 to 6
- layout_cotangent: bfloat16 [32, 512, 192], P(('dp', 'tensor')), may hold values from -6 to 6
Outputs:
- text_result: bfloat16 [32, 512, 768], P(('dp', 'tensor'))
- layout_result: bfloat16 [32, 512, 192], P(('dp', 'tensor'))
- text_gradient: float32 [32, 512, 768], P(('dp', 'tensor'))
- layout_gradient: float32 [32, 512, 192], P(('dp', 'tensor'))
- joint_text_gradient: float32 [768, 2304], replicated
- mixing_text_gradient: float32 [768, 768], replicated
- norms_text_gradient: float32 [4, 768], replicated
- upward_text_gradient: float32 [768, 3072], P(None, 'tensor')
- downward_text_gradient: float32 [3072, 768], P('tensor')
- joint_layout_gradient: float32 [192, 576], replicated
- mixing_layout_gradient: float32 [192, 192], replicated
- norms_layout_gradient: float32 [4, 192], replicated
- upward_layout_gradient: float32 [192, 768], P(None, 'tensor')
- downward_layout_gradient: float32 [768, 192], P('tensor')
The draws below stay inside these ranges and needn't reach their ends.
Inputs may be any that keep to these rules, and one draw needn't show every extreme that they name: `page_counts`: keys of a page in slots below its count are live; some page has all 512 slots live; counts are spread over several powers of two.
All inputs are finite; a program needn't handle non-finite values.
Results may differ from the reference program's by a relative error of at most 0.015.
Values may be sent and summed in bfloat16 or wider, within the bound.
No kernel may reach another device: no remote copies, remote signals or barrier semaphores. Data moves between devices by JAX's collectives and lax.ppermute only.
A program may use at most 192 MiB of HBM per device.

```python
import math
import jax
import jax.numpy as jnp
from jax import lax

HEADS = 12
FF_T = 3072
FF_L = 768
SLOTS = 512
D_T = 768
D_L = 192
PAGES = 32


def draw_page_counts(key, part):
    first, second, third = jax.random.split(key, 3)
    levels = jax.random.randint(first, (PAGES,), 0, 6)
    base = jnp.left_shift(jnp.full((PAGES,), SLOTS // 32, jnp.int32), levels.astype(jnp.int32))
    extra = jax.random.randint(second, (PAGES,), 0, base)
    counts = jnp.minimum(base + extra, SLOTS).astype(jnp.int32)
    chosen = jax.random.randint(third, (), 0, PAGES)
    return jnp.where(jnp.arange(PAGES) == chosen, SLOTS, counts).astype(jnp.int32)


def block_scale(rng, dims, pieces, least, high):
    level = 1.0
    for position, shards_of in pieces:
        draws = jax.random.uniform(jax.random.fold_in(jax.random.fold_in(rng, 6), position), (shards_of,), jnp.float32, least / len(pieces), high / len(pieces))
        level = level * jnp.repeat(jnp.exp(draws), dims[position] // shards_of).reshape((-1,) + (1,) * (len(dims) - 1 - position))
    return level


def gaussian(key, dims, scale, most, cuts=(), kind=jnp.bfloat16):
    drawn = scale * jax.random.normal(key, dims, jnp.float32)
    if cuts:
        drawn = drawn * block_scale(key, dims, cuts, -0.22, 0.18)
    return jnp.clip(drawn, -most, most).astype(kind)


def setup_inputs(seed: int = 0) -> dict:
    streams_of = jax.random.split(jax.random.key(seed), 16)
    return {
        "text_input": gaussian(streams_of[0], (PAGES, SLOTS, D_T), 1.0, 6.0, ((0, 32),)),
        "layout_input": gaussian(streams_of[1], (PAGES, SLOTS, D_L), 1.0, 6.0, ((0, 32),)),
        "page_counts": draw_page_counts(jax.random.fold_in(streams_of[15], 71), 0),
        "text_joint": gaussian(streams_of[3], (D_T, 3 * D_T), D_T ** -0.5, 0.21875),
        "text_mixing": gaussian(streams_of[4], (D_T, D_T), (D_T // 8) ** -0.5, 0.625),
        "text_norms": jnp.clip(1.0 + 0.18 * jax.random.normal(streams_of[5], (4, D_T), jnp.float32), 0.1, 1.9),
        "text_upward": gaussian(streams_of[6], (D_T, FF_T), D_T ** -0.5, 0.21875, ((1, 2),)),
        "text_downward": gaussian(streams_of[7], (FF_T, D_T), FF_T ** -0.5, 0.109375, ((0, 2),)),
        "layout_joint": gaussian(streams_of[8], (D_L, 3 * D_L), D_L ** -0.5, 0.4375),
        "layout_mixing": gaussian(streams_of[9], (D_L, D_L), (D_L // 8) ** -0.5, 1.25),
        "layout_norms": jnp.clip(1.0 + 0.18 * jax.random.normal(streams_of[10], (4, D_L), jnp.float32), 0.1, 1.9),
        "layout_upward": gaussian(streams_of[11], (D_L, FF_L), D_L ** -0.5, 0.4375, ((1, 2),)),
        "layout_downward": gaussian(streams_of[12], (FF_L, D_L), FF_L ** -0.5, 0.21875, ((0, 2),)),
        "text_cotangent": gaussian(streams_of[13], (PAGES, SLOTS, D_T), 1.0, 6.0, ((0, 32),)),
        "layout_cotangent": gaussian(streams_of[14], (PAGES, SLOTS, D_L), 1.0, 6.0, ((0, 32),)),
    }


@jax.custom_vjp
def low(v):
    return lax.optimization_barrier(v.astype(jnp.bfloat16)).astype(jnp.float32)

@jax.custom_vjp
def low_back(v):
    return v

def low_keep(v):
    return (low(v), None)

def low_pass(kept, grad):
    return (grad,)

def back_keep(v):
    return (v, None)

def back_low(kept, grad):
    return (low(grad),)
low.defvjp(low_keep, low_pass)
low_back.defvjp(back_keep, back_low)

def product(left, right):
    return jnp.dot(left, right, preferred_element_type=jnp.float32, precision=lax.Precision.HIGHEST)

def einsum_high(form, left, right):
    return jnp.einsum(form, left, right, preferred_element_type=jnp.float32, precision=lax.Precision.HIGHEST)

def both_ways(value):
    return low_back(low(value))

def normalize(hidden, gain, shift):
    center = hidden - lax.optimization_barrier(jnp.mean(hidden, axis=-1, keepdims=True))
    spread = lax.optimization_barrier(jnp.mean(center * center, axis=-1, keepdims=True))
    return center * lax.rsqrt(spread + 1e-05) * gain + shift

def split_joint(joint, pages, heads):
    slots = joint.shape[0] // pages
    grid = joint.reshape(pages, slots, 3, heads, joint.shape[1] // (3 * heads))
    return (grid[:, :, 0], grid[:, :, 1], grid[:, :, 2])

def path_tail(rows, attended, norms, upward, downward):
    first = normalize(rows + attended, norms[0], norms[1])
    hidden = low_back(product(low(first), upward))
    active = low(jax.nn.gelu(hidden, approximate=False))
    feed = low_back(product(active, downward))
    return normalize(first + feed, norms[2], norms[3])

def layer_group(text_rows, layout_rows, counts, fixed_queries, fixed_keys, text_joint, text_mixing, text_norms, text_upward, text_downward, layout_joint, layout_mixing, layout_norms, layout_upward, layout_downward):
    pages = counts.shape[0]
    slots = text_rows.shape[0] // pages
    text_query, text_key, text_value = split_joint(both_ways(product(low(text_rows), text_joint)), pages, HEADS)
    layout_query, layout_key, layout_value = split_joint(both_ways(product(low(layout_rows), layout_joint)), pages, HEADS)
    text_scale = 1.0 / math.sqrt(text_query.shape[-1])
    layout_scale = 1.0 / math.sqrt(layout_query.shape[-1])
    text_score = low_back(einsum_high('gqhd,gkhd->ghqk', text_query, text_key) * text_scale)
    layout_score = low_back(einsum_high('gqhd,gkhd->ghqk', layout_query, layout_key) * layout_scale)
    fixed_score = einsum_high('gqhd,gkhd->ghqk', fixed_queries, fixed_keys) * text_scale
    live = (jnp.arange(slots)[None, :] < counts[:, None])[:, None, None, :]
    text_logits = jnp.where(live, text_score + layout_score, -1e+30)
    layout_logits = jnp.where(live, layout_score + fixed_score, -1e+30)
    text_probs = low(jax.nn.softmax(text_logits, axis=-1))
    layout_probs = low(jax.nn.softmax(layout_logits, axis=-1))
    text_mixed = both_ways(einsum_high('ghqk,gkhd->gqhd', text_probs, text_value)).reshape(text_rows.shape)
    layout_mixed = both_ways(einsum_high('ghqk,gkhd->gqhd', layout_probs, layout_value)).reshape(layout_rows.shape)
    text_attended = low_back(product(text_mixed, text_mixing))
    layout_attended = low_back(product(layout_mixed, layout_mixing))
    return (path_tail(text_rows, text_attended, text_norms, text_upward, text_downward), path_tail(layout_rows, layout_attended, layout_norms, layout_upward, layout_downward))

def reference(text_input, layout_input, page_counts, text_joint, text_mixing, text_norms, text_upward, text_downward, layout_joint, layout_mixing, layout_norms, layout_upward, layout_downward, text_cotangent, layout_cotangent):
    weights = tuple((weight.astype(jnp.float32) for weight in (text_joint, text_mixing, text_norms, text_upward, text_downward, layout_joint, layout_mixing, layout_norms, layout_upward, layout_downward)))
    group = math.gcd(PAGES, max(1, 4096 // SLOTS))
    blocks = PAGES // group
    text_all = text_input.astype(jnp.float32).reshape(blocks, group * SLOTS, -1)
    layout_all = layout_input.astype(jnp.float32).reshape(blocks, group * SLOTS, -1)
    text_cots = text_cotangent.astype(jnp.float32).reshape(blocks, group * SLOTS, -1)
    layout_cots = layout_cotangent.astype(jnp.float32).reshape(blocks, group * SLOTS, -1)
    counts_all = page_counts.astype(jnp.int32).reshape(blocks, group)

    def step(totals, items):
        text_rows, layout_rows, counts, text_cot, layout_cot = items
        fixed = split_joint(low(product(low(text_rows), weights[0])), group, HEADS)

        def forward(text_x, layout_x, *params):
            return layer_group(text_x, layout_x, counts, fixed[0], fixed[1], *params)
        results, pullback = jax.vjp(forward, text_rows, layout_rows, *weights)
        grads = pullback((text_cot, layout_cot))
        totals = tuple((total + extra for total, extra in zip(totals, grads[2:])))
        return (totals, (results[0], results[1], grads[0], grads[1]))
    zeros = tuple((jnp.zeros(weight.shape, jnp.float32) for weight in weights))
    totals, outputs = lax.scan(step, zeros, (text_all, layout_all, counts_all, text_cots, layout_cots))
    text_result = outputs[0].reshape(PAGES, SLOTS, -1).astype(jnp.bfloat16)
    layout_result = outputs[1].reshape(PAGES, SLOTS, -1).astype(jnp.bfloat16)
    text_gradient = outputs[2].reshape(PAGES, SLOTS, -1)
    layout_gradient = outputs[3].reshape(PAGES, SLOTS, -1)
    return (text_result, layout_result, text_gradient, layout_gradient, totals[0], totals[1], totals[2], totals[3], totals[4], totals[5], totals[6], totals[7], totals[8], totals[9])
```

```python
import functools
import math

import jax
import jax.numpy as jnp
from jax import lax
from jax.experimental import pallas as pl
from jax.experimental.pallas import tpu as pltpu
from jax.sharding import PartitionSpec as P

HEADS = 12
NEG_FILL = -1e30
EPS = 1e-05
F32 = jnp.float32
BF16 = jnp.bfloat16
VMEM_SPEC = pl.BlockSpec(memory_space=pltpu.VMEM)
SMEM_SPEC = pl.BlockSpec(memory_space=pltpu.SMEM)
VMEM_LIMIT = 16 * 1024 * 1024


def nn(left, right):
    return lax.dot_general(left, right, (((1,), (0,)), ((), ())), preferred_element_type=F32)


def nt(left, right):
    return lax.dot_general(left, right, (((1,), (1,)), ((), ())), preferred_element_type=F32)


def tn(left, right):
    return lax.dot_general(left, right, (((0,), (0,)), ((), ())), preferred_element_type=F32)


def gelu_pair(hidden):
    below = 0.5 * (1.0 + lax.erf(hidden * math.sqrt(0.5)))
    bell = jnp.exp(-0.5 * hidden * hidden)
    return hidden * below, below + hidden * bell * (1.0 / math.sqrt(2.0 * math.pi))


def unit(hidden):
    center = hidden - jnp.mean(hidden, axis=-1, keepdims=True)
    spread = jnp.mean(center * center, axis=-1, keepdims=True)
    rate = lax.rsqrt(spread + EPS)
    return center * rate, rate


def unit_back(normed, rate, grad, gain):
    scaled = grad * gain
    return rate * (
        scaled
        - jnp.mean(scaled, axis=-1, keepdims=True)
        - normed * jnp.mean(scaled * normed, axis=-1, keepdims=True)
    )


def lane_masks(head, lane):
    base = (head // 8) * 8
    return (lane // 64) == (head % 2), (lane // 16) == (head - base)


PLAN_DOWN = ((1024, (0, 1, 2, 3)), (512, (2, 0, 1, 3)))
PLAN_UP = ((1152, (1, 2, 0, 3)), (576, (2, 0, 1, 3)))
PLAN_HALF = ((640, (0, 1, 2, 3)), (640, (1, 2, 0, 3)), (384, (2, 0, 1, 3)))


def pieces(plan, start, count):
    at, base = start, 0
    for rows, order in plan:
        leaf = rows // 8
        while base <= at < min(base + rows, start + count):
            which, offset = divmod(at - base, leaf)
            n = min(leaf - offset, start + count - at)
            yield at, n, base, leaf, which, offset, order
            at += n
        base += rows


def mask_of(sides, order):
    return sides[order[0]] * 4 + sides[order[1]] * 2 + sides[order[2]]


def spot_of(sides, plan, start, count):
    for at, n, base, leaf, which, offset, order in pieces(plan, start, count):
        row = base + offset + leaf * jnp.bitwise_xor(mask_of(sides, order), which)
        yield at - start, n, pl.multiple_of(row, math.gcd(math.gcd(base + offset, leaf), 64))


def place(out, sides, plan, start, value, columns=slice(None)):
    for at, n, row in spot_of(sides, plan, start, value.shape[0]):
        out[pl.ds(row, n), columns] = value[at:at + n, :]


def place_half(out, sides, plan, start, value, columns=slice(None)):
    half = sum(rows for rows, _ in plan)
    at = start
    while at < start + value.shape[0]:
        which, inner = divmod(at, half)
        count = min(half - inner, start + value.shape[0] - at)
        for off, n, row in spot_of(sides, plan, inner, count):
            there = pl.multiple_of(jnp.bitwise_xor(sides[4], which) * half + row, 16)
            out[pl.ds(there, n), columns] = value[at - start + off:at - start + off + n, :]
        at += count


def fetch(pairs, sems):
    copies = [pltpu.make_async_copy(src, dst, sems.at[i]) for i, (src, dst) in enumerate(pairs)]
    for copy in copies:
        copy.start()
    return copies


def front_kernel(
    count_ref, sides, text_any, layout_any, joint_t_any, joint_l_any, mix_t_any, mix_l_any,
    qkv_t, qkv_l, mixed_t, mixed_l, normed_t, normed_l, stats,
    text_ref, layout_ref, joint_t, joint_l, mix_t, mix_l, mix_acc, flipped, sems,
):
    slots, width_t = text_ref.shape
    width_l = layout_ref.shape[1]
    columns = [slice(j * width_t, (j + 1) * width_t) for j in range(3)]
    copies = fetch(
        [
            (layout_any.at[0], flipped), (joint_l_any, joint_l), (text_any.at[0], text_ref),
            *((joint_t_any.at[:, c], joint_t.at[:, c]) for c in columns),
            (mix_t_any, mix_t), (mix_l_any, mix_l),
        ],
        sems,
    )
    count = count_ref[0]
    mix_acc[...] = jnp.zeros_like(mix_acc)
    stats[...] = jnp.zeros_like(stats)
    copies[0].wait()
    copies[1].wait()
    layout_ref[...] = flipped[...].T
    for j in range(3):
        qkv_l[:, j * 256:j * 256 + width_l] = nn(
            layout_ref[...], joint_l[:, j * width_l:(j + 1) * width_l]
        ).astype(BF16)
        qkv_l[:, j * 256 + width_l:(j + 1) * 256] = jnp.zeros((slots, 256 - width_l), BF16)
    copies[2].wait()
    for j, c in enumerate(columns):
        copies[3 + j].wait()
        qkv_t[:, c] = nn(text_ref[...], joint_t[:, c]).astype(BF16)
    lane = lax.broadcasted_iota(jnp.int32, (slots, 128), 1)
    dead = lax.broadcasted_iota(jnp.int32, (slots, slots), 1) >= count

    def pair_step(pair, carry):
        spot = lambda start: pl.ds(pl.multiple_of(start, 128), 128)
        at_l = (pair // 4) * 128
        query_t, key_t, value_t = (qkv_t[:, spot(j * width_t + pair * 128)] for j in range(3))
        query_l, key_l, value_l = (qkv_l[:, spot(j * 256 + at_l)] for j in range(3))
        keys = jnp.concatenate([key_t, key_l], axis=1)
        values = jnp.concatenate([value_t, value_l], axis=1)
        for side in range(2):
            head = 2 * pair + side
            mask_t, mask_l = lane_masks(head, lane)
            queries = jnp.concatenate(
                [
                    jnp.where(mask_t, query_t * 0.125, 0),
                    jnp.where(mask_l, query_l * 0.25, 0),
                ],
                axis=1,
            ).astype(BF16)
            logits = jnp.where(dead, NEG_FILL, nt(queries, keys))
            top = jnp.max(logits, axis=1, keepdims=True)
            raised = jnp.exp(logits - top)
            mass = jnp.sum(raised, axis=1, keepdims=True)
            stats[...] = jnp.where(lane == head, top + jnp.log(mass), stats[...])
            out = nn(raised.astype(BF16), values) * (1.0 / mass)
            if side == 0:
                first = out[:, :128]
            else:
                mixed_t[:, spot(pair * 128)] = jnp.where(mask_t, out[:, :128], first).astype(BF16)
            mix_acc[:, spot(at_l)] = mix_acc[:, spot(at_l)] + jnp.where(mask_l, out[:, 128:], 0.0)
        return carry

    lax.fori_loop(0, HEADS // 2, pair_step, 0)
    mixed_l[...] = mix_acc[:, :width_l].astype(BF16)
    copies[6].wait()
    normed, rate = unit(text_ref[...].astype(F32) + nn(mixed_t[...], mix_t[...]))
    normed_t[...] = normed
    stats[...] = jnp.where(lane == 16, rate, stats[...])
    copies[7].wait()
    normed, rate = unit(layout_ref[...].astype(F32) + nn(mixed_l[...], mix_l[...]))
    normed_l[...] = normed
    stats[...] = jnp.where(lane == 17, rate, stats[...])


def column(stats, lane, which):
    return jnp.sum(jnp.where(lane == which, stats[...], 0.0), axis=1, keepdims=True)


ANY_SPEC = pl.BlockSpec(memory_space=pltpu.HBM)


def call(kernel, micros, outs, args, scratch=(), specs=None, aliases=None, limit=16):
    moved = sum(math.prod(a.shape) * a.dtype.itemsize for a in args)
    return pl.pallas_call(
        kernel,
        out_shape=[(pltpu.VMEM(s, d) if kept else jax.ShapeDtypeStruct(s, d)) for s, d, kept in outs],
        in_specs=specs or [VMEM_SPEC] * len(args),
        out_specs=[VMEM_SPEC] * len(outs),
        scratch_shapes=list(scratch),
        input_output_aliases=aliases or {},
        compiler_params=pltpu.CompilerParams(vmem_limit_bytes=limit * 1024 * 1024),
        cost_estimate=pl.CostEstimate(flops=int(micros * 1.1e9), bytes_accessed=moved, transcendentals=0),
    )(*args)


def front(count, sides, text, layout, joint_t, joint_l, mix_t, mix_l):
    _, s, wt = text.shape
    wl = layout.shape[1]
    return call(
        front_kernel,
        12,
        [
            ((s, 3 * wt), BF16, True), ((s, 768), BF16, True), ((s, wt), BF16, True), ((s, wl), BF16, True),
            ((s, wt), F32, True), ((s, wl), F32, True), ((s, 128), F32, True),
        ],
        (count, sides, text, layout, joint_t, joint_l, mix_t, mix_l),
        [
            pltpu.VMEM((s, wt), BF16), pltpu.VMEM((s, wl), BF16), pltpu.VMEM((wt, 3 * wt), BF16),
            pltpu.VMEM((wl, 3 * wl), BF16), pltpu.VMEM((wt, wt), BF16), pltpu.VMEM((wl, wl), BF16),
            pltpu.VMEM((s, 256), F32), pltpu.VMEM((wl, s), BF16), pltpu.SemaphoreType.DMA((8,)),
        ],
        [SMEM_SPEC] * 2 + [ANY_SPEC] * 6,
        limit=56,
    )


def feed_kernel(
    sides, normed_t, normed_l, norms_t, norms_l, cot_t, cot_l,
    up_t0, up_t1, down_t0, down_t1, up_l0, up_l1, down_l0, down_l1,
    result_t, result_l, second_t, second_l, dfeed_t, dfeed_l, low_t, low_l,
    act_t0, act_t1, slope_t0, slope_t1, act_l0, act_l1, slope_l0, slope_l1,
    dnorm_t, dnorm_l, down_far,
):
    step = 512
    cuts = [slice(at, at + step) for at in range(0, up_t0.shape[1], step)]
    first_t = normed_t[...] * norms_t[0:1, :] + norms_t[1:2, :]
    low_t[...] = first_t.astype(BF16)
    first_l = normed_l[...] * norms_l[0:1, :] + norms_l[1:2, :]
    low_l[...] = first_l.astype(BF16)
    for up, act, slope in ((up_t0, act_t0, slope_t0), (up_t1, act_t1, slope_t1)):
        for cut in cuts:
            active, rise = gelu_pair(nn(low_t[...], up[:, cut]))
            act[:, cut] = active.astype(BF16)
            slope[:, cut] = rise.astype(BF16)
    for up, act, slope in ((up_l0, act_l0, slope_l0), (up_l1, act_l1, slope_l1)):
        active, rise = gelu_pair(nn(low_l[...], up[...]))
        act[...] = active.astype(BF16)
        slope[...] = rise.astype(BF16)
    summed_l = first_l + nt(act_l0[...], down_l0[...]) + nt(act_l1[...], down_l1[...])
    summed_t = normed_t[...] * norms_t[0:1, :] + norms_t[1:2, :] + (
        nn(act_t0[...], down_t0[...]) + nn(act_t1[...], down_t1[...])
    )
    for summed, norms, cot, result, second, dfeed, dnorm in (
        (summed_t, norms_t, cot_t, result_t, second_t, dfeed_t, dnorm_t),
        (summed_l, norms_l, cot_l, result_l, second_l, dfeed_l, dnorm_l),
    ):
        normed, rate = unit(summed)
        value = (normed * norms[2:3, :] + norms[3:4, :]).astype(BF16)
        result[...] = value if result is result_t else value.T
        grad = (cot[0] if cot is cot_t else cot[0].T).astype(F32)
        dnorm[0:1, :] = jnp.sum(grad * normed, axis=0, keepdims=True)
        dnorm[1:2, :] = jnp.sum(grad, axis=0, keepdims=True)
        back = unit_back(normed, rate, grad, norms[2:3, :])
        second[...] = back
        dfeed[...] = back.astype(BF16)
    down_kernel(sides, act_t1, dfeed_t, down_far)


def feed(sides, normed_t, normed_l, norms_t, norms_l, cot_t, cot_l, weights):
    s, wt = normed_t.shape
    wl = normed_l.shape[1]
    ht, hl = weights[0].shape[1], weights[4].shape[1]
    return call(
        feed_kernel,
        16,
        [((s, wt), BF16, False), ((wl, s), BF16, False)]
        + [((s, wt), F32, True), ((s, wl), F32, True)]
        + [((s, wt), BF16, True), ((s, wl), BF16, True)] * 2
        + [((s, ht), BF16, True)] * 4
        + [((s, hl), BF16, True)] * 4
        + [((2, wt), F32, True), ((2, wl), F32, True), ((ht, wt), BF16, False)],
        (sides, normed_t, normed_l, norms_t, norms_l, cot_t, cot_l) + tuple(weights),
        specs=[SMEM_SPEC] + [VMEM_SPEC] * 14,
        limit=16,
    )


def down_kernel(sides, act, dfeed, out):
    step = 512
    for start in range(0, act.shape[1], step):
        place(out, sides, PLAN_DOWN, start, tn(act[:, start:start + step], dfeed[...]).astype(BF16))


def up_body(
    sides, dfeed_t, dfeed_l, low_t, low_l, down_t, down_l, slope_t, slope_l, act_l, up_t, up_l, prev_t, prev_l,
    grads, dfirst_t, dfirst_l, dhid,
):
    wt = low_t.shape[1]
    wl = low_l.shape[1]
    for start in range(0, down_t.shape[0], wt):
        at = slice(start, start + wt)
        dhid[:, at] = (nt(dfeed_t[...], down_t[at, :]) * slope_t[:, at].astype(F32)).astype(BF16)
        place(grads, sides, PLAN_UP, start, tn(low_t[...], dhid[:, at]).astype(BF16))
    dfirst_t[...] = prev_t[...] + nt(dhid[...], up_t[...])
    base = down_t.shape[0]
    hl = down_l.shape[1]
    dhidden = (nn(dfeed_l[...], down_l[...]) * slope_l[...].astype(F32)).astype(BF16)
    lower = tn(act_l[...], dfeed_l[...]).astype(BF16)
    packed = jnp.concatenate([tn(low_l[...], dhidden).astype(BF16), lower[:wl, :], lower[wl:, :]], axis=1)
    place(grads, sides, PLAN_UP, base, packed)
    dfirst_l[...] = prev_l[...] + nt(dhidden, up_l[...])


def up_kernel(*refs):
    up_body(*refs)


def up_down_kernel(*refs):
    sides, act_t, refs = refs[0], refs[1], refs[2:]
    down_kernel(sides, act_t, refs[0], refs[13])
    up_body(sides, *refs[:13], *refs[14:])


def up_grad(sides, act_t, *args):
    dfeed_t, dfeed_l, low_t, low_l, down_t = args[:5]
    s, wt = low_t.shape
    wl = low_l.shape[1]
    ht = down_t.shape[0]
    outs = [((ht + wl, wt), BF16, False), ((s, wt), F32, True), ((s, wl), F32, True)]
    scratch = [pltpu.VMEM((s, ht), BF16)]
    if act_t is None:
        specs = [SMEM_SPEC] + [VMEM_SPEC] * len(args)
        return call(up_kernel, 5, outs, (sides,) + args, scratch, specs)
    specs = [SMEM_SPEC] + [VMEM_SPEC] * (len(args) + 1)
    return call(up_down_kernel, 8, [((ht, wt), BF16, False)] + outs, (sides, act_t) + args, scratch, specs)


def turn_kernel(
    sides, mixed_t, mixed_l, normed_t, normed_l, stats, dfirst_t, dfirst_l, norms_t, norms_l, dnorm_t, dnorm_l, mix_t, mix_l,
    grads, dtext, dlayout, dmix_t, dmix_l, mix_low,
):
    slots, wt = mixed_t.shape
    wl = mixed_l.shape[1]
    base = 4 * wt
    lane = lax.broadcasted_iota(jnp.int32, (slots, 128), 1)
    norm_row = base + wl
    kept = []
    for n, (first, normed, norms, dnorm, width, mixed, mix, dmix) in enumerate((
        (dfirst_t, normed_t, norms_t, dnorm_t, wt, mixed_t, mix_t, dmix_t),
        (dfirst_l, normed_l, norms_l, dnorm_l, wl, mixed_l, mix_l, dmix_l),
    )):
        grad = first[...]
        unitv = normed[...]
        gain_grad = jnp.sum(grad * unitv, axis=0, keepdims=True)
        shift_grad = jnp.sum(grad, axis=0, keepdims=True)
        rows = jnp.concatenate([gain_grad, shift_grad, dnorm[0:2, :]], axis=0)
        kept.append(jnp.concatenate(
            [rows.astype(BF16), jnp.zeros((12, width), BF16)], axis=0
        ) if width == wt else jnp.concatenate(
            [jnp.concatenate([rows.astype(BF16), jnp.zeros((4, wt - width), BF16)], axis=1), jnp.zeros((44, wt), BF16)],
            axis=0,
        ))
        resid = unit_back(unitv, column(stats, lane, 16 + n), grad, norms[0:1, :])
        low = resid.astype(BF16)
        if n == 0:
            dtext[...] = resid
            place_half(grads, sides, PLAN_HALF, 3 * wt, tn(mixed[...], low).astype(BF16))
            dmix[...] = nt(low, mix[...]).astype(BF16)
        else:
            dlayout[...] = resid
            mix_low[...] = tn(mixed[...], low).astype(BF16)
            dmix[:, :wl] = nt(low, mix[...]).astype(BF16)
            dmix[:, wl:] = jnp.zeros((slots, 256 - wl), BF16)
    place_half(grads, sides, PLAN_HALF, norm_row, jnp.concatenate(kept, axis=0))


def turn(*args):
    s, wt = args[1].shape
    wl = args[2].shape[1]
    rows = 4 * wt + wl + 64
    return call(
        turn_kernel,
        4,
        [
            ((rows, wt), BF16, True), ((s, wt), F32, True), ((s, wl), F32, True), ((s, wt), BF16, True),
            ((s, 256), BF16, True), ((wl, wl), BF16, True),
        ],
        args,
        specs=[SMEM_SPEC] + [VMEM_SPEC] * (len(args) - 1),
    )


def pairs_kernel(lo, hi, fresh, count_ref, qkv_t, qkv_l, stats, dmix_t, dmix_l, *refs):
    djoint_t, acc_l = refs[-2:]
    slots, wt = dmix_t.shape
    count = count_ref[0]
    if fresh:
        acc_l[...] = jnp.zeros_like(acc_l)
    lane = lax.broadcasted_iota(jnp.int32, (slots, 128), 1)
    dead = lax.broadcasted_iota(jnp.int32, (slots, slots), 1) >= count

    def pair_step(pair, carry):
        spot = lambda start: pl.ds(pl.multiple_of(start, 128), 128)
        at_l = (pair // 4) * 128
        query_t, key_t, value_t = (qkv_t[:, spot(j * wt + pair * 128)] for j in range(3))
        query_l, key_l, value_l = (qkv_l[:, spot(j * 256 + at_l)] for j in range(3))
        upper_t = dmix_t[:, spot(pair * 128)]
        upper_l = dmix_l[:, spot(at_l)]
        keys = jnp.concatenate([key_t, key_l], axis=1)
        values = jnp.concatenate([value_t, value_l], axis=1)
        kept = None
        for side in range(2):
            head = 2 * pair + side
            mask_t, mask_l = lane_masks(head, lane)
            queries = jnp.concatenate(
                [
                    jnp.where(mask_t, query_t * 0.125, 0),
                    jnp.where(mask_l, query_l * 0.25, 0),
                ],
                axis=1,
            ).astype(BF16)
            logits = jnp.where(dead, NEG_FILL, nt(queries, keys))
            probs = jnp.exp(logits - column(stats, lane, head))
            own_t = jnp.where(mask_t, upper_t, 0).astype(BF16)
            own_l = jnp.where(mask_l, upper_l, 0).astype(BF16)
            grad_t = nt(own_t, value_t)
            grad_s = nt(jnp.concatenate([own_t, own_l], axis=1), values)
            score_t = (probs * (grad_t - jnp.sum(grad_t * probs, axis=1, keepdims=True))).astype(BF16)
            score_l = (probs * (grad_s - jnp.sum(grad_s * probs, axis=1, keepdims=True))).astype(BF16)
            dvalue = tn(probs.astype(BF16), jnp.concatenate([upper_t, upper_l], axis=1))
            dquery_t = nn(score_t, key_t) * 0.125
            dkey_t = tn(score_t, query_t) * 0.125
            dquery_l = nn(score_l, key_l) * 0.25
            dkey_l = tn(score_l, query_l) * 0.25
            if side == 0:
                kept = (dquery_t, dkey_t, dvalue[:, :128])
            else:
                for j, (old, new) in enumerate(zip(kept, (dquery_t, dkey_t, dvalue[:, :128]))):
                    djoint_t[:, spot(j * wt + pair * 128)] = jnp.where(mask_t, new, old).astype(BF16)
            for j, part in enumerate((dquery_l, dkey_l, dvalue[:, 128:])):
                at = spot(j * 256 + at_l)
                acc_l[:, at] = acc_l[:, at] + jnp.where(mask_l, part, 0.0)
        return carry

    lax.fori_loop(lo, hi, pair_step, 0)


def pairs(lo, hi, prev, *args):
    s, wt = args[4].shape
    outs = [((s, 3 * wt), BF16, True), ((s, 768), F32, True)]
    n = len(args)
    return call(
        functools.partial(pairs_kernel, lo, hi, prev is None),
        3 * (hi - lo),
        outs,
        args + tuple(prev or ()),
        specs=[SMEM_SPEC] + [VMEM_SPEC] * (n - 1 + (2 if prev else 0)),
        aliases={n: 0, n + 1: 1} if prev else None,
    )


def close_kernel(
    sides, text_ref, layout_ref, djoint_t, acc_l, joint_t, joint_l, mix_low, part_ref, dtext_in, dlayout_in,
    grads, dtext, dlayout, djoint_l,
):
    wt = text_ref.shape[2]
    wl = layout_ref.shape[1]
    base = 4 * wt

    for j in range(3):
        place_half(
            grads, sides, PLAN_HALF, j * wt, tn(text_ref[0], djoint_t[:, j * wt:(j + 1) * wt]).astype(BF16)
        )
    for j in range(3):
        djoint_l[:, j * wl:(j + 1) * wl] = acc_l[:, j * 256:j * 256 + wl].astype(BF16)
    low = jnp.concatenate([nn(layout_ref[0], djoint_l[...]).astype(BF16), mix_low[...]], axis=1)
    place_half(grads, sides, PLAN_HALF, base, low)
    dtext[...] = dtext_in[...] + nt(djoint_t[...], joint_t[...])
    dlayout[...] = (dlayout_in[...] + nt(djoint_l[...], joint_l[...])).T


def close(*args):
    text, layout = args[1:3]
    _, s, wt = text.shape
    wl = layout.shape[1]
    return call(
        close_kernel,
        5,
        [(args[8].shape, BF16, True), ((s, wt), F32, False), ((wl, s), F32, False)],
        args,
        [pltpu.VMEM((s, 3 * wl), BF16)],
        specs=[SMEM_SPEC] + [VMEM_SPEC] * (len(args) - 1),
        aliases={8: 0},
    )


AXES = ("dp", "tensor")


def swap(value, bit, many):
    dp, tensor = many
    pairs = []
    for d in range(dp):
        for t in range(tensor):
            to = (d, t ^ 1) if bit < 0 else (d ^ (1 << bit), t)
            pairs.append((d * tensor + t, to[0] * tensor + to[1]))
    return lax.ppermute(value, AXES, pairs)


def cut_of(value, base, rows):
    return lax.slice_in_dim(value, base, base + rows, axis=0)


def tie(values, *others):
    got = lax.optimization_barrier((tuple(values), tuple(others)))
    return got[0]


class Stream:
    def __init__(self, plan, own, got, many):
        self.plan, self.many = plan, many
        self.keep, self.send, base = [], [], 0
        for rows, _ in plan:
            half = rows // 2
            self.keep.append(cut_of(own, base, half) + cut_of(got, base, half))
            self.send.append(cut_of(own, base + half, half) + cut_of(got, base + half, half))
            base += rows

    def reduce(self, step):
        got = [swap(v, order[step], self.many) for v, (_, order) in zip(self.send, self.plan)]
        keep, send = [], []
        for k, g in zip(self.keep, got):
            if step < 2:
                half = k.shape[0] // 2
                keep.append(cut_of(k, 0, half) + cut_of(g, 0, half))
                send.append(cut_of(k, half, half) + cut_of(g, half, half))
            else:
                keep.append(k + g)
        self.keep, self.send = keep, send

    def cross(self):
        whole = jnp.concatenate(self.keep, axis=0)
        whole = whole + swap(whole, self.plan[0][1][3], self.many)
        base, keep = 0, []
        for k in self.keep:
            keep.append(cut_of(whole, base, k.shape[0]))
            base += k.shape[0]
        self.keep = keep

    def spread(self, step):
        got = [swap(v, order[step], self.many) for v, (_, order) in zip(self.keep, self.plan)]
        if step:
            self.keep = [jnp.concatenate([k, g], axis=0) for k, g in zip(self.keep, got)]
        else:
            self.keep = [(k, g) for k, g in zip(self.keep, got)]

    def flat(self):
        return [part for pair in self.keep for part in pair]


def read_rows(parts, sides, plan, start, count):
    bases = {}
    base = 0
    for i, (rows, _) in enumerate(plan):
        bases[base] = i
        base += rows
    for at, n, base, leaf, which, offset, order in pieces(plan, start, count):
        pair = parts[2 * bases[base]], parts[2 * bases[base] + 1]
        rel = jnp.bitwise_xor(mask_of(sides, order), which)
        row = pl.multiple_of(jnp.bitwise_and(rel, 3) * leaf + offset, math.gcd(math.gcd(leaf, offset), 64))
        yield at - start, n, pair, rel < 4, row


def move(parts, sides, plan, start, count, write):
    for at, n, pair, low, row in read_rows(parts, sides, plan, start, count):
        for ref, here in zip(pair, (low, jnp.logical_not(low))):

            @pl.when(here)
            def _(ref=ref, at=at, n=n, row=row):
                write(at, n, ref[pl.ds(row, n), :].astype(F32))


def put(out, column, width):
    def write(at, n, value):
        out[at:at + n, column:column + width] = value[:, :width]

    return write


def open_down_kernel(sides, *refs):
    parts, out = refs[:-1], refs[-1]
    move(parts, sides, PLAN_DOWN, 0, out.shape[0], put(out, 0, out.shape[1]))


def open_up_kernel(sides, *refs):
    parts, (up_t, up_l, down_l) = refs[:-3], refs[-3:]
    wt, hidden = up_t.shape
    wl, hl = up_l.shape
    for column in range(0, hidden, wt):
        move(parts, sides, PLAN_UP, column, wt, put(up_t, column, wt))

    def low(at, n, value):
        up_l[at:at + n, :] = value[:, :hl]
        down_l[at:at + n, :] = value[:, hl:hl + wl]
        down_l[wl + at:wl + at + n, :] = value[:, hl + wl:]

    move(parts, sides, PLAN_UP, hidden, wl, low)


def open_half_kernel(sides, *refs):
    count = 2 * len(PLAN_HALF)
    own, other, (joint_t, mix_t, norm_t, joint_l, mix_l, norm_l) = refs[:count], refs[count:2 * count], refs[2 * count:]
    wt, wl = mix_t.shape[0], mix_l.shape[0]
    half = sum(rows for rows, _ in PLAN_HALF)

    def low(at, n, value):
        joint_l[at:at + n, :] = value[:, :3 * wl]
        mix_l[at:at + n, :] = value[:, 3 * wl:]

    def norm(out, width):
        def write(at, n, value):
            out[...] = value[:4, :width]

        return write

    fields = [(j * wt, wt, put(joint_t, j * wt, wt)) for j in range(3)]
    fields += [(3 * wt, wt, put(mix_t, 0, wt)), (4 * wt, wl, low)]
    fields += [(4 * wt + wl, 16, norm(norm_t, wt)), (4 * wt + wl + 16, 16, norm(norm_l, wl))]
    for core in range(2):

        @pl.when(sides[4] == core)
        def _():
            for which in range(2):
                parts = own if which == core else other
                for start, rows, write in fields:
                    lo, hi = max(start, which * half), min(start + rows, (which + 1) * half)
                    if lo < hi:
                        move(
                            parts, sides, PLAN_HALF, lo - which * half, hi - lo,
                            lambda at, n, value, shift=lo - start, write=write: write(at + shift, n, value),
                        )


def open_up(kernel, micros, outs, sides, parts):
    return call(
        kernel, micros, [(shape, F32, False) for shape in outs], (sides,) + tuple(parts),
        specs=[SMEM_SPEC] + [VMEM_SPEC] * len(parts),
    )


def shards(
    many, text_input, layout_input, page_counts, text_joint, text_mixing, text_norms, text_upward, text_downward,
    layout_joint, layout_mixing, layout_norms, layout_upward, layout_downward, text_cotangent, layout_cotangent,
):
    dp, tensor = many
    wt, wl = text_input.shape[2], layout_input.shape[2]
    layout_flip = layout_input.swapaxes(1, 2)
    halves = tensor == 2 and dp == 16
    own = (text_upward, text_downward, layout_upward, layout_downward.T)
    if halves:
        far = tuple(swap(w, -1, many) for w in own)
    else:
        whole = [
            lax.all_gather(w, "tensor", axis=axis, tiled=True) for w, axis in zip(own, (1, 0, 1, 1))
        ]
        cut = lambda w, axis, i: lax.slice_in_dim(w, i * (w.shape[axis] // 2), (i + 1) * (w.shape[axis] // 2), axis=axis)
        own = tuple(cut(w, axis, 0) for w, axis in zip(whole, (1, 0, 1, 1)))
        far = tuple(cut(w, axis, 1) for w, axis in zip(whole, (1, 0, 1, 1)))
    place_bits = lax.axis_index("dp").astype(jnp.int32)
    sides = jnp.stack([(place_bits >> b) & 1 for b in range(4)] + [lax.axis_index("tensor").astype(jnp.int32) & 1])
    if not halves:
        sides = jnp.zeros_like(sides)
    (
        qkv_t, qkv_l, mixed_t, mixed_l, normed_t, normed_l, stats,
    ) = front(page_counts, sides, text_input, layout_flip, text_joint, layout_joint, text_mixing, layout_mixing)
    up_t0, down_t0, up_l0, down_l0 = own
    up_t1, down_t1, up_l1, down_l1 = far
    (
        result_t, result_l, second_t, second_l, dfeed_t, dfeed_l, low_t, low_l,
        act_t0, act_t1, slope_t0, slope_t1, act_l0, act_l1, slope_l0, slope_l1, dnorm_t, dnorm_l, down_far,
    ) = feed(
        sides, normed_t, normed_l, text_norms, layout_norms, text_cotangent, layout_cotangent.swapaxes(1, 2),
        (own[0], far[0], own[1], far[1], own[2], far[2], own[3], far[3]),
    )
    down_got = swap(down_far, -1, many) if halves else None
    down_own, up_far, dfirst_t, dfirst_l = up_grad(
        sides, act_t0,
        dfeed_t, dfeed_l, low_t, low_l, down_t1, down_l1, slope_t1, slope_l1, act_l1, up_t1, up_l1, second_t, second_l
    )
    if halves:
        up_got = swap(up_far, -1, many)
        down = Stream(PLAN_DOWN, down_own, down_got, many)
        dfirst_t, = tie([dfirst_t], *down.send)
    up_own, dfirst_t, dfirst_l = up_grad(
        sides, None,
        dfeed_t, dfeed_l, low_t, low_l, down_t0, down_l0, slope_t0, slope_l0, act_l0, up_t0, up_l0, dfirst_t, dfirst_l
    )
    if halves:
        up = Stream(PLAN_UP, up_own, up_got, many)
        dfirst_t, = tie([dfirst_t], *up.send)
    grads, dtext, dlayout, dmix_t, dmix_l, mix_low = turn(
        sides, mixed_t, mixed_l, normed_t, normed_l, stats, dfirst_t, dfirst_l, text_norms, layout_norms, dnorm_t, dnorm_l,
        text_mixing, layout_mixing,
    )
    state = None
    for lo in range(0, HEADS // 2, 2):
        if halves and lo == 2:
            down.reduce(0)
            dmix_t, = tie([dmix_t], *down.send)
        if halves and lo == 4:
            up.reduce(0)
            down.reduce(1)
            dmix_t, = tie([dmix_t], *up.send, *down.send)
        state = pairs(lo, lo + 2, state, page_counts, qkv_t, qkv_l, stats, dmix_t, dmix_l)
    if halves:
        up.reduce(1)
        down.reduce(2)
        state = tie(state, *up.send, *down.keep)
    grads, dtext, dlayout = close(
        sides, text_input, layout_flip, state[0], state[1], text_joint, layout_joint, mix_low, grads, dtext, dlayout
    )

    def unpack_up(packed, hidden, hl):
        text_part = jnp.concatenate([packed[i * wt:(i + 1) * wt] for i in range(hidden // wt)], axis=1)
        low_part = packed[hidden:]
        return text_part, low_part[:, :hl], jnp.concatenate([low_part[:, hl:hl + wl], low_part[:, hl + wl:]], axis=0)

    if halves:
        rows = grads.shape[0] // 2
        half = Stream(PLAN_HALF, cut_of(grads, 0, rows), swap(cut_of(grads, rows, rows), -1, many), many)
        down.cross()
        up.reduce(2)
        up.cross()
        for step in range(3):
            half.reduce(step)
        half.cross()
        for stream in (down, up, half):
            for step in (2, 1, 0):
                stream.spread(step)
        own_parts = half.flat()
        far_parts = [swap(part, -1, many) for part in own_parts]
        ht, hl = text_upward.shape[1], layout_upward.shape[1]
        down_grad_t, = open_up(open_down_kernel, 3, [(ht, wt)], sides, down.flat())
        up_grad_t, up_grad_l, down_grad_l = open_up(
            open_up_kernel, 3, [(wt, ht), (wl, hl), (hl, wl)], sides, up.flat()
        )
        joint_t, mix_t, norm_t, joint_l, mix_l, norm_l = open_up(
            open_half_kernel, 5, [(wt, 3 * wt), (wt, wt), (4, wt), (wl, 3 * wl), (wl, wl), (4, wl)],
            sides, own_parts + far_parts,
        )
    else:
        hidden = down_own.shape[0]
        parts = [unpack_up(up, hidden, up_l0.shape[1]) for up in (up_own, up_far)]
        joined = [
            jnp.concatenate([parts[0][0], parts[1][0]], axis=1),
            jnp.concatenate([down_own, down_far], axis=0),
            jnp.concatenate([parts[0][1], parts[1][1]], axis=1),
            jnp.concatenate([parts[0][2], parts[1][2]], axis=0),
        ]
        up_grad_t, down_grad_t, up_grad_l, down_grad_l = (
            lax.psum(lax.psum_scatter(g, "tensor", scatter_dimension=axis, tiled=True), "dp")
            for g, axis in zip(joined, (1, 0, 1, 0))
        )
        grads = lax.psum(grads, AXES).astype(F32)
        low = grads[4 * wt:4 * wt + wl]
        rows = 4 * wt + wl
        joint_t, mix_t = jnp.concatenate([grads[j * wt:(j + 1) * wt] for j in range(3)], axis=1), grads[3 * wt:4 * wt]
        norm_t, norm_l = grads[rows:rows + 4], grads[rows + 16:rows + 20, :wl]
        joint_l, mix_l = low[:, :3 * wl], low[:, 3 * wl:]
    return (
        result_t[None],
        result_l.T[None],
        dtext[None],
        dlayout.T[None],
        joint_t,
        mix_t,
        norm_t,
        up_grad_t.astype(F32),
        down_grad_t.astype(F32),
        joint_l,
        mix_l,
        norm_l,
        up_grad_l.astype(F32),
        down_grad_l.astype(F32),
    )


def solution(mesh):
    many = (mesh.shape["dp"], mesh.shape["tensor"])
    pages = P(("dp", "tensor"), None, None)
    columns, rows = P(None, "tensor"), P("tensor", None)
    return jax.shard_map(
        functools.partial(shards, many),
        mesh=mesh,
        in_specs=(
            pages, pages, P(("dp", "tensor")), P(), P(), P(), columns, rows, P(), P(), P(), columns, rows, pages, pages,
        ),
        out_specs=(
            pages, pages, pages, pages, P(), P(), P(), columns, rows, P(), P(), P(), columns, rows,
        ),
        check_vma=False,
    )
```

```python
import functools
import math

import jax
import jax.numpy as jnp
from jax import lax
from jax.experimental import pallas as pl
from jax.experimental.pallas import tpu as pltpu
from jax.sharding import PartitionSpec as P

HEADS = 12
NEG_FILL = -1e30
EPS = 1e-05
F32 = jnp.float32
BF16 = jnp.bfloat16
VMEM_SPEC = pl.BlockSpec(memory_space=pltpu.VMEM)
SMEM_SPEC = pl.BlockSpec(memory_space=pltpu.SMEM)
SCALE = 1.0


def nn(left, right):
    return lax.dot_general(left, right, (((1,), (0,)), ((), ())), preferred_element_type=F32)


def nt(left, right):
    return lax.dot_general(left, right, (((1,), (1,)), ((), ())), preferred_element_type=F32)


def tn(left, right):
    return lax.dot_general(left, right, (((0,), (0,)), ((), ())), preferred_element_type=F32)


def gelu_pair(hidden):
    below = 0.5 * (1.0 + lax.erf(hidden * math.sqrt(0.5)))
    bell = jnp.exp(-0.5 * hidden * hidden)
    return hidden * below, below + hidden * bell * (1.0 / math.sqrt(2.0 * math.pi))


def unit(hidden):
    center = hidden - jnp.mean(hidden, axis=-1, keepdims=True)
    spread = jnp.mean(center * center, axis=-1, keepdims=True)
    rate = lax.rsqrt(spread + EPS)
    return center * rate, rate


def unit_back(normed, rate, grad, gain):
    scaled = grad * gain
    return rate * (
        scaled
        - jnp.mean(scaled, axis=-1, keepdims=True)
        - normed * jnp.mean(scaled * normed, axis=-1, keepdims=True)
    )


def lane_masks(head, lane):
    base = (head // 8) * 8
    return (lane // 64) == (head % 2), (lane // 16) == (head - base)


ORDERS = (((0, 2, 1, 3), (1, 0, 2, 3)), ((1, 2, 0, 3), (2, 0, 1, 3)), ((0, 2, 1, 3), (2, 0, 1, 3)), ((0, 1, 2, 3), (1, 0, 2, 3)))
FIELDS_DOWN = ((("down", 0, 192),),)
FIELDS_UP = ((("left", 0, 96), ("right", 0, 96), ("low", 0, 32)),)
FIELDS_HALF = (
    (("query", 0, 32), ("key", 0, 32), ("value", 0, 16), ("mix", 0, 16), ("low", 0, 16)),
    (("query", 256, 16), ("key", 256, 16), ("value", 128, 32), ("mix", 128, 32)),
)
PLANS = (FIELDS_DOWN, FIELDS_UP, FIELDS_HALF)
HALF_ROWS = {"query": 384, "key": 384, "value": 384, "mix": 384, "low": 128}
EVENTS = (
    "B2", "D.core", "B3", "U.core", "turn", "p0", "p1", "D0.0", "p2", "U0.0", "D0.1", "close", "in", "D0.2",
    "U0.1", "A.core", "U0.2", "D0.3", "A1.0", "A0.0", "A1.1", "U0.3", "D0.4", "A0.1", "A1.2", "U0.4", "A0.2",
    "D0.5", "A1.3", "A0.3", "A1.4", "U0.5", "A0.4", "D0.6", "oD", "A1.5", "A0.5", "A1.6", "A0.6", "U0.6",
    "oU",
)


def leaf_of(fields):
    return sum(n for _, _, n in fields)


def streams_of(plan):
    base = 0
    first = sum(len(p) for p in PLANS[:PLANS.index(plan)])
    for i, fields in enumerate(plan):
        yield first + i, base, leaf_of(fields), fields
        base += 8 * leaf_of(fields)


def rows_of(plan):
    return sum(8 * leaf_of(fields) for fields in plan)


def sides_of(dp, tensor):
    bits = [(dp >> b) & 1 for b in range(4)]
    values = [tensor & 1]
    for orders in ORDERS:
        values += [bits[o[0]] * 4 + bits[o[1]] * 2 + bits[o[2]] for o in orders]
    return jnp.stack(values)


def place(out, sides, core, plan, field, value, start=0, shift=0, columns=slice(None)):
    for number, base, leaf, fields in streams_of(plan):
        mask = sides[1 + 2 * number + core]
        inner = 0
        for name, first, n in fields:
            if name == field:
                for l in range(8):
                    at = first + l * n - start
                    if 0 <= at < value.shape[0]:
                        row = shift + base + inner + leaf * jnp.bitwise_xor(mask, l)
                        row = pl.multiple_of(row, math.gcd(math.gcd(base + inner, leaf), 16))
                        out[pl.ds(row, n), columns] = value[at:at + n, :]
            inner += n


def place_half(out, sides, field, value):
    half = HALF_ROWS[field]
    for core in range(2):
        shift = jnp.bitwise_xor(sides[0], core) * rows_of(FIELDS_HALF)
        place(out, sides, core, FIELDS_HALF, field, value[core * half:(core + 1) * half, :], 0, shift)


def fetch(pairs, sems):
    copies = [pltpu.make_async_copy(src, dst, sems.at[i]) for i, (src, dst) in enumerate(pairs)]
    for copy in copies:
        copy.start()
    return copies


def front_kernel(
    count_ref, sides, text_any, layout_any, joint_t_any, joint_l_any, mix_t_any, mix_l_any,
    qkv_t, qkv_l, mixed_t, mixed_l, normed_t, normed_l, stats,
    text_ref, layout_ref, joint_t, joint_l, mix_t, mix_l, mix_acc, flipped, sems,
):
    slots, width_t = text_ref.shape
    width_l = layout_ref.shape[1]
    columns = [slice(j * width_t, (j + 1) * width_t) for j in range(3)]
    copies = fetch(
        [
            (layout_any.at[0], flipped), (joint_l_any, joint_l), (text_any.at[0], text_ref),
            *((joint_t_any.at[:, c], joint_t.at[:, c]) for c in columns),
            (mix_t_any, mix_t), (mix_l_any, mix_l),
        ],
        sems,
    )
    count = count_ref[0]
    mix_acc[...] = jnp.zeros_like(mix_acc)
    stats[...] = jnp.zeros_like(stats)
    copies[0].wait()
    copies[1].wait()
    layout_ref[...] = flipped[...].T
    for j in range(3):
        qkv_l[:, j * 256:j * 256 + width_l] = nn(
            layout_ref[...], joint_l[:, j * width_l:(j + 1) * width_l]
        ).astype(BF16)
        qkv_l[:, j * 256 + width_l:(j + 1) * 256] = jnp.zeros((slots, 256 - width_l), BF16)
    copies[2].wait()
    for j, c in enumerate(columns):
        copies[3 + j].wait()
        qkv_t[:, c] = nn(text_ref[...], joint_t[:, c]).astype(BF16)
    lane = lax.broadcasted_iota(jnp.int32, (slots, 128), 1)
    dead = lax.broadcasted_iota(jnp.int32, (slots, slots), 1) >= count

    def pair_step(pair, carry):
        spot = lambda start: pl.ds(pl.multiple_of(start, 128), 128)
        at_l = (pair // 4) * 128
        query_t, key_t, value_t = (qkv_t[:, spot(j * width_t + pair * 128)] for j in range(3))
        query_l, key_l, value_l = (qkv_l[:, spot(j * 256 + at_l)] for j in range(3))
        keys = jnp.concatenate([key_t, key_l], axis=1)
        values = jnp.concatenate([value_t, value_l], axis=1)
        for side in range(2):
            head = 2 * pair + side
            mask_t, mask_l = lane_masks(head, lane)
            queries = jnp.concatenate(
                [
                    jnp.where(mask_t, query_t * 0.125, 0),
                    jnp.where(mask_l, query_l * 0.25, 0),
                ],
                axis=1,
            ).astype(BF16)
            logits = jnp.where(dead, NEG_FILL, nt(queries, keys))
            top = jnp.max(logits, axis=1, keepdims=True)
            raised = jnp.exp(logits - top)
            mass = jnp.sum(raised, axis=1, keepdims=True)
            stats[...] = jnp.where(lane == head, top + jnp.log(mass), stats[...])
            out = nn(raised.astype(BF16), values) * (1.0 / mass)
            if side == 0:
                first = out[:, :128]
            else:
                mixed_t[:, spot(pair * 128)] = jnp.where(mask_t, out[:, :128], first).astype(BF16)
            mix_acc[:, spot(at_l)] = mix_acc[:, spot(at_l)] + jnp.where(mask_l, out[:, 128:], 0.0)
        return carry

    lax.fori_loop(0, HEADS // 2, pair_step, 0)
    mixed_l[...] = mix_acc[:, :width_l].astype(BF16)
    copies[6].wait()
    normed, rate = unit(text_ref[...].astype(F32) + nn(mixed_t[...], mix_t[...]))
    normed_t[...] = normed
    stats[...] = jnp.where(lane == 16, rate, stats[...])
    copies[7].wait()
    normed, rate = unit(layout_ref[...].astype(F32) + nn(mixed_l[...], mix_l[...]))
    normed_l[...] = normed
    stats[...] = jnp.where(lane == 17, rate, stats[...])


def column(stats, lane, which):
    return jnp.sum(jnp.where(lane == which, stats[...], 0.0), axis=1, keepdims=True)


ANY_SPEC = pl.BlockSpec(memory_space=pltpu.HBM)


def call(kernel, micros, outs, args, scratch=(), specs=None, aliases=None, limit=16, out_specs=None):
    moved = sum(math.prod(a.shape) * a.dtype.itemsize for a in args)
    return pl.pallas_call(
        kernel,
        out_shape=[(pltpu.VMEM(s, d) if kept else jax.ShapeDtypeStruct(s, d)) for s, d, kept in outs],
        in_specs=specs or [VMEM_SPEC] * len(args),
        out_specs=out_specs or [VMEM_SPEC] * len(outs),
        scratch_shapes=list(scratch),
        input_output_aliases=aliases or {},
        compiler_params=pltpu.CompilerParams(vmem_limit_bytes=limit * 1024 * 1024),
        cost_estimate=pl.CostEstimate(flops=int(micros * SCALE * 1.1e9), bytes_accessed=moved, transcendentals=0),
    )(*args)


def front(count, sides, text, layout, joint_t, joint_l, mix_t, mix_l):
    _, s, wt = text.shape
    wl = layout.shape[1]
    return call(
        front_kernel,
        12,
        [
            ((s, 3 * wt), BF16, True), ((s, 768), BF16, True), ((s, wt), BF16, True), ((s, wl), BF16, True),
            ((s, wt), F32, True), ((s, wl), F32, True), ((s, 128), F32, True),
        ],
        (count, sides, text, layout, joint_t, joint_l, mix_t, mix_l),
        [
            pltpu.VMEM((s, wt), BF16), pltpu.VMEM((s, wl), BF16), pltpu.VMEM((wt, 3 * wt), BF16),
            pltpu.VMEM((wl, 3 * wl), BF16), pltpu.VMEM((wt, wt), BF16), pltpu.VMEM((wl, wl), BF16),
            pltpu.VMEM((s, 256), F32), pltpu.VMEM((wl, s), BF16), pltpu.SemaphoreType.DMA((8,)),
        ],
        [SMEM_SPEC] * 2 + [ANY_SPEC] * 6,
        limit=56,
    )


def feed_kernel(
    sides, normed_t, normed_l, norms_t, norms_l, *refs,
):
    far_refs, refs = refs[:10], refs[10:]
    (
        result_t, result_l, second_t, second_l, dfeed_t, dfeed_l, low_t, low_l,
        act_t0, act_t1, slope_t0, slope_t1, act_l0, act_l1, slope_l0, slope_l1,
        dnorm_t, dnorm_l, down_far,
    ) = refs[:19]
    cot_t, cot_l, up_t0, up_t1, down_t0, down_t1, up_l0, up_l1, down_l0, down_l1 = far_refs
    step = 512
    cuts = [slice(at, at + step) for at in range(0, up_t0.shape[1], step)]
    first_t = normed_t[...] * norms_t[0:1, :] + norms_t[1:2, :]
    low_t[...] = first_t.astype(BF16)
    first_l = normed_l[...] * norms_l[0:1, :] + norms_l[1:2, :]
    low_l[...] = first_l.astype(BF16)
    for up, act, slope in ((up_t0, act_t0, slope_t0), (up_t1, act_t1, slope_t1)):
        for cut in cuts:
            active, rise = gelu_pair(nn(low_t[...], up[:, cut]))
            act[:, cut] = active.astype(BF16)
            slope[:, cut] = rise.astype(BF16)
    for up, act, slope in ((up_l0, act_l0, slope_l0), (up_l1, act_l1, slope_l1)):
        active, rise = gelu_pair(nn(low_l[...], up[...]))
        act[...] = active.astype(BF16)
        slope[...] = rise.astype(BF16)
    summed_l = first_l + nt(act_l0[...], down_l0[...]) + nt(act_l1[...], down_l1[...])
    summed_t = normed_t[...] * norms_t[0:1, :] + norms_t[1:2, :] + (
        nn(act_t0[...], down_t0[...]) + nn(act_t1[...], down_t1[...])
    )
    for summed, norms, cot, result, second, dfeed, dnorm in (
        (summed_t, norms_t, cot_t, result_t, second_t, dfeed_t, dnorm_t),
        (summed_l, norms_l, cot_l, result_l, second_l, dfeed_l, dnorm_l),
    ):
        normed, rate = unit(summed)
        value = (normed * norms[2:3, :] + norms[3:4, :]).astype(BF16)
        result[...] = value if result is result_t else value.T
        grad = (cot[0] if cot is cot_t else cot[0].T).astype(F32)
        dnorm[0:1, :] = jnp.sum(grad * normed, axis=0, keepdims=True)
        dnorm[1:2, :] = jnp.sum(grad, axis=0, keepdims=True)
        back = unit_back(normed, rate, grad, norms[2:3, :])
        second[...] = back
        dfeed[...] = back.astype(BF16)
    down_kernel(sides, 1, act_t1, dfeed_t, down_far)


def feed(sides, normed_t, normed_l, norms_t, norms_l, cot_t, cot_l, weights):
    s, wt = normed_t.shape
    wl = normed_l.shape[1]
    ht, hl = weights[0].shape[1], weights[4].shape[1]
    return call(
        feed_kernel,
        16,
        [((s, wt), BF16, False), ((wl, s), BF16, False)]
        + [((s, wt), F32, True), ((s, wl), F32, True)]
        + [((s, wt), BF16, True), ((s, wl), BF16, True)] * 2
        + [((s, ht), BF16, True)] * 4
        + [((s, hl), BF16, True)] * 4
        + [((2, wt), F32, True), ((2, wl), F32, True), ((ht, wt), BF16, False)],
        (sides, normed_t, normed_l, norms_t, norms_l, cot_t, cot_l) + tuple(weights),
        specs=[SMEM_SPEC] + [VMEM_SPEC] * 14,
        limit=16,
    )


def down_kernel(sides, far, act, dfeed, out):
    core = jnp.bitwise_xor(sides[0], far)
    step = 768
    for start in range(0, act.shape[1], step):
        place(out, sides, core, FIELDS_DOWN, "down", tn(act[:, start:start + step], dfeed[...]).astype(BF16), start)


def up_body(
    sides, far, dfeed_t, dfeed_l, low_t, low_l, down_t, down_l, slope_t, slope_l, act_l, up_t, up_l, prev_t, prev_l,
    grads, dfirst_t, dfirst_l, dhid,
):
    wt = low_t.shape[1]
    wl = low_l.shape[1]
    core = jnp.bitwise_xor(sides[0], far)
    for start in range(0, down_t.shape[0], wt):
        at = slice(start, start + wt)
        dhid[:, at] = (nt(dfeed_t[...], down_t[at, :]) * slope_t[:, at].astype(F32)).astype(BF16)
        field = "right" if start else "left"
        place(grads, sides, core, FIELDS_UP, field, tn(low_t[...], dhid[:, at]).astype(BF16))
    dfirst_t[...] = prev_t[...] + nt(dhid[...], up_t[...])
    hl = down_l.shape[1]
    dhidden = (nn(dfeed_l[...], down_l[...]) * slope_l[...].astype(F32)).astype(BF16)
    lower = tn(act_l[...], dfeed_l[...]).astype(BF16)
    packed = jnp.concatenate([tn(low_l[...], dhidden).astype(BF16), lower[:wl, :], lower[wl:, :]], axis=1)
    place(grads, sides, core, FIELDS_UP, "low", jnp.concatenate([packed, jnp.zeros((64, wt), BF16)], axis=0))
    dfirst_l[...] = prev_l[...] + nt(dhidden, up_l[...])


def up_kernel(sides, *refs):
    up_body(sides, 0, *refs)


def up_down_kernel(*refs):
    sides, act_t, refs = refs[0], refs[1], refs[2:]
    down_kernel(sides, 0, act_t, refs[0], refs[13])
    up_body(sides, 1, *refs[:13], *refs[14:])


def up_grad(sides, act_t, *args):
    dfeed_t, dfeed_l, low_t, low_l, down_t = args[:5]
    s, wt = low_t.shape
    wl = low_l.shape[1]
    ht = down_t.shape[0]
    outs = [((ht + wl + 64, wt), BF16, False), ((s, wt), F32, True), ((s, wl), F32, True)]
    scratch = [pltpu.VMEM((s, ht), BF16)]
    if act_t is None:
        specs = [SMEM_SPEC] + [VMEM_SPEC] * len(args)
        return call(up_kernel, 5, outs, (sides,) + args, scratch, specs)
    specs = [SMEM_SPEC] + [VMEM_SPEC] * (len(args) + 1)
    return call(up_down_kernel, 8, [((ht, wt), BF16, False)] + outs, (sides, act_t) + args, scratch, specs)


def turn_kernel(
    sides, mixed_t, mixed_l, normed_t, normed_l, stats, dfirst_t, dfirst_l, norms_t, norms_l, dnorm_t, dnorm_l, mix_t, mix_l,
    grads, dtext, dlayout, dmix_t, dmix_l, mix_low, norm_low, djoint_t, acc_l,
):
    slots, wt = mixed_t.shape
    wl = mixed_l.shape[1]
    acc_l[...] = jnp.zeros_like(acc_l)
    djoint_t[...] = jnp.zeros_like(djoint_t)
    lane = lax.broadcasted_iota(jnp.int32, (slots, 128), 1)
    kept = []
    for n, (first, normed, norms, dnorm, width, mixed, mix, dmix) in enumerate((
        (dfirst_t, normed_t, norms_t, dnorm_t, wt, mixed_t, mix_t, dmix_t),
        (dfirst_l, normed_l, norms_l, dnorm_l, wl, mixed_l, mix_l, dmix_l),
    )):
        grad = first[...]
        unitv = normed[...]
        gain_grad = jnp.sum(grad * unitv, axis=0, keepdims=True)
        shift_grad = jnp.sum(grad, axis=0, keepdims=True)
        rows = jnp.concatenate([gain_grad, shift_grad, dnorm[0:2, :]], axis=0)
        kept.append(jnp.concatenate(
            [rows.astype(BF16), jnp.zeros((12, width), BF16)], axis=0
        ) if width == wt else jnp.concatenate(
            [jnp.concatenate([rows.astype(BF16), jnp.zeros((4, wt - width), BF16)], axis=1), jnp.zeros((44, wt), BF16)],
            axis=0,
        ))
        resid = unit_back(unitv, column(stats, lane, 16 + n), grad, norms[0:1, :])
        low = resid.astype(BF16)
        if n == 0:
            dtext[...] = resid
            place_half(grads, sides, "mix", tn(mixed[...], low).astype(BF16))
            dmix[...] = nt(low, mix[...]).astype(BF16)
        else:
            dlayout[...] = resid
            mix_low[...] = tn(mixed[...], low).astype(BF16)
            dmix[:, :wl] = nt(low, mix[...]).astype(BF16)
            dmix[:, wl:] = jnp.zeros((slots, 256 - wl), BF16)
    norm_low[...] = jnp.concatenate(kept, axis=0)


def turn(*args):
    s, wt = args[1].shape
    wl = args[2].shape[1]
    rows = 4 * wt + wl + 64
    return call(
        turn_kernel,
        4,
        [
            ((rows, wt), BF16, True), ((s, wt), F32, True), ((s, wl), F32, True), ((s, wt), BF16, True),
            ((s, 256), BF16, True), ((wl, wl), BF16, True), ((64, wt), BF16, True), ((s, 3 * wt), BF16, True),
            ((s, 768), F32, True),
        ],
        args,
        specs=[SMEM_SPEC] + [VMEM_SPEC] * (len(args) - 1),
    )


def pairs_kernel(span_ref, count_ref, qkv_t, qkv_l, stats, dmix_t, dmix_l, djoint_in, acc_in, djoint_t, acc_l):
    slots, wt = dmix_t.shape
    count = count_ref[0]
    lane = lax.broadcasted_iota(jnp.int32, (slots, 128), 1)
    dead = lax.broadcasted_iota(jnp.int32, (slots, slots), 1) >= count

    def pair_step(pair, carry):
        spot = lambda start: pl.ds(pl.multiple_of(start, 128), 128)
        at_l = (pair // 4) * 128
        query_t, key_t, value_t = (qkv_t[:, spot(j * wt + pair * 128)] for j in range(3))
        query_l, key_l, value_l = (qkv_l[:, spot(j * 256 + at_l)] for j in range(3))
        upper_t = dmix_t[:, spot(pair * 128)]
        upper_l = dmix_l[:, spot(at_l)]
        keys = jnp.concatenate([key_t, key_l], axis=1)
        values = jnp.concatenate([value_t, value_l], axis=1)
        kept = None
        for side in range(2):
            head = 2 * pair + side
            mask_t, mask_l = lane_masks(head, lane)
            queries = jnp.concatenate(
                [
                    jnp.where(mask_t, query_t * 0.125, 0),
                    jnp.where(mask_l, query_l * 0.25, 0),
                ],
                axis=1,
            ).astype(BF16)
            logits = jnp.where(dead, NEG_FILL, nt(queries, keys))
            probs = jnp.exp(logits - column(stats, lane, head))
            own_t = jnp.where(mask_t, upper_t, 0).astype(BF16)
            own_l = jnp.where(mask_l, upper_l, 0).astype(BF16)
            grad_t = nt(own_t, value_t)
            grad_s = nt(jnp.concatenate([own_t, own_l], axis=1), values)
            score_t = (probs * (grad_t - jnp.sum(grad_t * probs, axis=1, keepdims=True))).astype(BF16)
            score_l = (probs * (grad_s - jnp.sum(grad_s * probs, axis=1, keepdims=True))).astype(BF16)
            dvalue = tn(probs.astype(BF16), jnp.concatenate([upper_t, upper_l], axis=1))
            dquery_t = nn(score_t, key_t) * 0.125
            dkey_t = tn(score_t, query_t) * 0.125
            dquery_l = nn(score_l, key_l) * 0.25
            dkey_l = tn(score_l, query_l) * 0.25
            if side == 0:
                kept = (dquery_t, dkey_t, dvalue[:, :128])
            else:
                for j, (old, new) in enumerate(zip(kept, (dquery_t, dkey_t, dvalue[:, :128]))):
                    djoint_t[:, spot(j * wt + pair * 128)] = jnp.where(mask_t, new, old).astype(BF16)
            for j, part in enumerate((dquery_l, dkey_l, dvalue[:, 128:])):
                at = spot(j * 256 + at_l)
                acc_l[:, at] = acc_l[:, at] + jnp.where(mask_l, part, 0.0)
        return carry

    lax.fori_loop(span_ref[0], span_ref[1], pair_step, 0)


def pairs(lo, hi, prev, *args):
    s, wt = args[4].shape
    span = jnp.array([lo, hi], jnp.int32)
    return call(
        pairs_kernel,
        3 * (hi - lo),
        [((s, 3 * wt), BF16, True), ((s, 768), F32, True)],
        (span,) + args + tuple(prev),
        specs=[SMEM_SPEC] * 2 + [VMEM_SPEC] * 7,
        aliases={7: 0, 8: 1},
    )


def close_kernel(
    sides, text_ref, layout_ref, djoint_t, acc_l, mix_low, norm_low, part_ref,
    grads, djoint_l,
):
    wt = text_ref.shape[2]
    wl = layout_ref.shape[1]
    for j, field in enumerate(("query", "key", "value")):
        place_half(grads, sides, field, tn(text_ref[0], djoint_t[:, j * wt:(j + 1) * wt]).astype(BF16))
    for j in range(3):
        djoint_l[:, j * wl:(j + 1) * wl] = acc_l[:, j * 256:j * 256 + wl].astype(BF16)
    low = jnp.concatenate([nn(layout_ref[0], djoint_l[...]).astype(BF16), mix_low[...]], axis=1)
    place_half(grads, sides, "low", jnp.concatenate([low, norm_low[...]], axis=0))


def close(*args):
    text, layout = args[1:3]
    _, s, wt = text.shape
    wl = layout.shape[1]
    return call(
        close_kernel,
        3,
        [(args[7].shape, BF16, True), ((s, 3 * wl), BF16, True)],
        args,
        specs=[SMEM_SPEC] + [VMEM_SPEC] * (len(args) - 1),
        aliases={7: 0},
    )


def inputs_kernel(djoint_t, djoint_l, joint_t, joint_l, dtext_in, dlayout_in, dtext, dlayout):
    dtext[...] = dtext_in[...] + nt(djoint_t[...], joint_t[...])
    dlayout[...] = (dlayout_in[...] + nt(djoint_l[...], joint_l[...])).T


def input_grads(*args):
    s, wt = args[4].shape
    wl = args[5].shape[1]
    return call(inputs_kernel, 3, [((s, wt), F32, False), ((wl, s), F32, False)], args)


AXES = ("dp", "tensor")


def swap(value, bits, many):
    dp, tensor = many
    pairs = []
    for d in range(dp):
        for t in range(tensor):
            to = (d, t ^ 1) if bits == -1 else (d ^ (1 << bits[t]), t)
            pairs.append((d * tensor + t, to[0] * tensor + to[1]))
    return lax.ppermute(value, AXES, pairs)


def cut_of(value, base, rows):
    return lax.slice_in_dim(value, base, base + rows, axis=0)


def tie(values, *others):
    got = lax.optimization_barrier((tuple(values), tuple(others)))
    return got[0]


class Stream:
    def __init__(self, fields, orders, many):
        self.half, self.orders, self.many = 4 * leaf_of(fields), orders, many

    def launch(self, phase, value):
        bits = tuple(order[min(phase, 6 - phase)] for order in self.orders)
        self.flying = swap(value, bits, self.many)
        return [value]

    def begin(self, own, got, base):
        half = self.half
        self.keep = cut_of(own, base, half) + cut_of(got, base, half)
        return self.launch(0, cut_of(own, base + half, half) + cut_of(got, base + half, half))

    def finish(self, phase, token):
        got, = tie([self.flying], *token)
        keep = self.keep
        if phase < 2:
            half = keep.shape[0] // 2
            self.keep = cut_of(keep, 0, half) + cut_of(got, 0, half)
            return self.launch(phase + 1, cut_of(keep, half, half) + cut_of(got, half, half))
        if phase == 6:
            self.keep = (keep, got)
            return [got]
        self.keep = keep + got if phase < 4 else jnp.concatenate([keep, got], axis=0)
        return self.launch(phase + 1, self.keep)


def unplace(parts, sides, core, plan, field, out, half=0):
    for i, (number, _, leaf, fields) in enumerate(streams_of(plan)):
        mask = sides[1 + 2 * number + core]
        inner = 0
        for name, first, n in fields:
            if name == field:
                for side in range(2):
                    part = parts[2 * i + side]

                    def copy(r, carry, first=first, n=n, inner=inner, part=part, mask=mask, side=side, leaf=leaf):
                        row = core * half + first + n * jnp.bitwise_xor(mask, 4 * side + r)
                        source = pl.ds(pl.multiple_of(inner + r * leaf, 16), n)
                        out[pl.ds(pl.multiple_of(row, 16), n), :] = part[source, :].astype(F32)
                        return carry

                    lax.fori_loop(0, 4, copy, 0)
            inner += n


def stage(refs, sems, fill):
    flying = []
    for i, (field, out, columns, buffer) in enumerate(refs):
        fill(field, buffer)
        copy = pltpu.make_async_copy(buffer, out.at[:, columns], sems.at[i])
        copy.start()
        flying.append(copy)
    return flying


def open_down_kernel(sides, *refs):
    parts, (out, buffer, sems) = refs[:-3], refs[-3:]
    unplace(parts, sides, sides[0], FIELDS_DOWN, "down", buffer)
    copy = pltpu.make_async_copy(buffer, out, sems.at[0])
    copy.start()
    copy.wait()


def open_up_kernel(sides, *refs):
    parts, (up_t, up_l, down_l, left, right, low, sems) = refs[:-7], refs[-7:]
    wt = up_t.shape[0]
    wl, hl = up_l.shape
    fill = functools.partial(unplace, parts, sides, sides[0], FIELDS_UP)
    flying = stage(
        [("left", up_t, slice(0, wt), left), ("right", up_t, slice(wt, 2 * wt), right)], sems, fill
    )
    fill("low", low)
    up_l[...] = low[:wl, :hl]
    down_l[:wl, :] = low[:wl, hl:hl + wl]
    down_l[wl:, :] = low[:wl, hl + wl:]
    for copy in flying:
        copy.wait()


def open_half_kernel(sides, *refs):
    count = 2 * len(FIELDS_HALF)
    own, other, refs = refs[:count], refs[count:2 * count], refs[2 * count:]
    joint_t, mix_t, joint_l, mix_l, norm_t, norm_l, *buffers, low, sems = refs
    wt, wl = mix_t.shape[0], mix_l.shape[0]

    def fill(field, out):
        for parts, core in ((own, sides[0]), (other, 1 - sides[0])):
            unplace(parts, sides, core, FIELDS_HALF, field, out, HALF_ROWS[field])

    outs = [(field, joint_t, slice(j * wt, (j + 1) * wt)) for j, field in enumerate(("query", "key", "value"))]
    flying = stage([(*o, b) for o, b in zip(outs + [("mix", mix_t, slice(0, wt))], buffers)], sems, fill)
    fill("low", low)
    joint_l[...] = low[:wl, :3 * wl]
    mix_l[...] = low[:wl, 3 * wl:]
    norm_t[...] = low[wl:wl + 4, :]
    norm_l[...] = low[wl + 16:wl + 20, :wl]
    for copy in flying:
        copy.wait()


def open_up(kernel, micros, direct, outs, buffers, sides, token, parts):
    if token:
        parts = [tie([parts[0]], *token)[0], *parts[1:]]
    return call(
        kernel, micros, [(shape, F32, False) for shape in outs], (sides,) + tuple(parts),
        [pltpu.VMEM(shape, F32) for shape in buffers] + [pltpu.SemaphoreType.DMA((4,))],
        [SMEM_SPEC] + [VMEM_SPEC] * len(parts), limit=24,
        out_specs=[ANY_SPEC] * direct + [VMEM_SPEC] * (len(outs) - direct),
    )


def shards(
    many, text_input, layout_input, page_counts, text_joint, text_mixing, text_norms, text_upward, text_downward,
    layout_joint, layout_mixing, layout_norms, layout_upward, layout_downward, text_cotangent, layout_cotangent,
):
    dp, tensor = many
    wt, wl = text_input.shape[2], layout_input.shape[2]
    layout_flip = layout_input.swapaxes(1, 2)
    halves = tensor == 2 and dp == 16
    own = (text_upward, text_downward, layout_upward, layout_downward.T)
    if halves:
        far = tuple(swap(w, -1, many) for w in own)
    else:
        whole = [
            lax.all_gather(w, "tensor", axis=axis, tiled=True) for w, axis in zip(own, (1, 0, 1, 1))
        ]
        cut = lambda w, axis, i: lax.slice_in_dim(w, i * (w.shape[axis] // 2), (i + 1) * (w.shape[axis] // 2), axis=axis)
        own = tuple(cut(w, axis, 0) for w, axis in zip(whole, (1, 0, 1, 1)))
        far = tuple(cut(w, axis, 1) for w, axis in zip(whole, (1, 0, 1, 1)))
    sides = sides_of(lax.axis_index("dp").astype(jnp.int32), lax.axis_index("tensor").astype(jnp.int32))
    if not halves:
        sides = jnp.zeros_like(sides)
    (
        qkv_t, qkv_l, mixed_t, mixed_l, normed_t, normed_l, stats,
    ) = front(page_counts, sides, text_input, layout_flip, text_joint, layout_joint, text_mixing, layout_mixing)
    up_t0, down_t0, up_l0, down_l0 = own
    up_t1, down_t1, up_l1, down_l1 = far
    (
        result_t, result_l, second_t, second_l, dfeed_t, dfeed_l, low_t, low_l,
        act_t0, act_t1, slope_t0, slope_t1, act_l0, act_l1, slope_l0, slope_l1, dnorm_t, dnorm_l, down_far,
    ) = feed(
        sides, normed_t, normed_l, text_norms, layout_norms, text_cotangent, layout_cotangent.swapaxes(1, 2),
        (own[0], far[0], own[1], far[1], own[2], far[2], own[3], far[3]),
    )
    run = {"token": [dfeed_t], "state": None, "first": (second_t, second_l)}
    streams = {
        "%s%d" % (name, number - first): Stream(fields, ORDERS[number], many)
        for name, plan in zip("DUA", PLANS)
        for first in [sum(len(p) for p in PLANS[:PLANS.index(plan)])]
        for number, _, _, fields in streams_of(plan)
    }
    got = {}
    if halves:
        got["D"] = swap(down_far, -1, many)

    def held(value):
        return tie([value], *run["token"])[0]

    def far_grads():
        down_own, up_far, *run["first"] = up_grad(
            sides, act_t0, held(dfeed_t),
            dfeed_l, low_t, low_l, down_t1, down_l1, slope_t1, slope_l1, act_l1, up_t1, up_l1, *run["first"]
        )
        run["down_own"], run["up_far"], run["token"] = down_own, up_far, [run["first"][0]]
        if halves:
            got["U"] = swap(up_far, -1, many)

    def own_grads():
        run["up_own"], *run["first"] = up_grad(
            sides, None, held(dfeed_t),
            dfeed_l, low_t, low_l, down_t0, down_l0, slope_t0, slope_l0, act_l0, up_t0, up_l0, *run["first"]
        )
        run["token"] = [run["first"][0]]

    def turn_back():
        run["grads"], run["dtext"], run["dlayout"], run["dmix_t"], run["dmix_l"], run["mix_low"], run["norm_low"], *run["state"] = turn(
            sides, mixed_t, mixed_l, normed_t, normed_l, stats, held(run["first"][0]), run["first"][1], text_norms,
            layout_norms, dnorm_t, dnorm_l, text_mixing, layout_mixing,
        )
        run["token"] = [run["dmix_t"]]

    def pair_grads(lo, hi):
        run["state"] = pairs(
            lo, hi, run["state"], page_counts, qkv_t, qkv_l, stats, held(run["dmix_t"]), run["dmix_l"]
        )
        run["token"] = [run["state"][1]]

    def close_up():
        state = run["state"]
        run["grads"], run["djoint_l"] = close(
            sides, text_input, layout_flip, state[0], held(state[1]), run["mix_low"], run["norm_low"], run["grads"],
        )
        run["token"] = [run["djoint_l"]]
        if halves:
            rows = run["grads"].shape[0] // 2
            run["half_own"] = cut_of(run["grads"], 0, rows)
            got["A"] = swap(cut_of(run["grads"], rows, rows), -1, many)

    def inputs_up():
        run["dtext"], run["dlayout"] = input_grads(
            run["state"][0], held(run["djoint_l"]), text_joint, layout_joint, run["dtext"], run["dlayout"]
        )
        run["token"] = [run["dlayout"]]

    ht, hl = text_upward.shape[1], layout_upward.shape[1]

    def parts_of(name, plan):
        return [part for i in range(len(plan)) for part in streams["%s%d" % (name, i)].keep]

    def open_down():
        run["down"] = open_up(open_down_kernel, 3, 1, [(ht, wt)], [(ht, wt)], sides, run["token"], parts_of("D", FIELDS_DOWN))
        run["token"] = list(run["down"])

    def open_upper():
        run["up"] = open_up(
            open_up_kernel, 3, 1, [(wt, ht), (wl, hl), (hl, wl)], [(wt, wt)] * 2 + [(256, wt)], sides, run["token"], parts_of("U", FIELDS_UP)
        )
        run["token"] = list(run["up"])

    kernels = {
        "B2": far_grads, "B3": own_grads, "turn": turn_back, "p0": lambda: pair_grads(0, 2),
        "p1": lambda: pair_grads(2, 4), "p2": lambda: pair_grads(4, 6), "close": close_up, "in": inputs_up,
    }
    opens = {"oD": open_down, "oU": open_upper}
    owns = {"D": ("down_own", FIELDS_DOWN), "U": ("up_own", FIELDS_UP), "A": ("half_own", FIELDS_HALF)}
    for event in EVENTS if halves else [e for e in EVENTS if e in kernels]:
        if event in kernels:
            kernels[event]()
        elif event in opens:
            opens[event]()
        else:
            name, step = event.split(".")
            if step == "core":
                here, = tie([got[name]], *run["token"])
                own_of, plan = owns[name]
                run["token"], base = [], 0
                for i, fields in enumerate(plan):
                    run["token"] += streams["%s%d" % (name, i)].begin(run[own_of], here, base)
                    base += 8 * leaf_of(fields)
            else:
                run["token"] = streams[name].finish(int(step), run["token"])
    grads, dtext, dlayout = run["grads"], run["dtext"], run["dlayout"]
    down_own, up_own, up_far = run["down_own"], run["up_own"], run["up_far"]

    if halves:
        own_parts = parts_of("A", FIELDS_HALF)
        far_parts = [swap(part, -1, many) for part in own_parts]
        down_grad_t, = run["down"]
        up_grad_t, up_grad_l, down_grad_l = run["up"]
        joint_t, mix_t, joint_l, mix_l, norm_t, norm_l = open_up(
            open_half_kernel, 4, 2, [(wt, 3 * wt), (wt, wt), (wl, 3 * wl), (wl, wl), (4, wt), (4, wl)],
            [(wt, wt)] * 4 + [(256, wt)], sides, [], own_parts + far_parts,
        )
    else:
        def parts(packed, plan, shift=0):
            return [
                cut_of(packed, shift + base + i * 4 * leaf, 4 * leaf)
                for _, base, leaf, _ in streams_of(plan) for i in range(2)
            ]

        hidden, wide = down_own.shape[0], up_l0.shape[1]
        downs = [
            open_up(open_down_kernel, 3, 1, [(hidden, wt)], [(hidden, wt)], sides, [], parts(p, FIELDS_DOWN))[0]
            for p in (down_own, down_far)
        ]
        ups = [
            open_up(
                open_up_kernel, 3, 1, [(wt, hidden), (wl, wide), (wide, wl)], [(wt, wt)] * 2 + [(256, wt)], sides, [],
                parts(p, FIELDS_UP),
            )
            for p in (up_own, up_far)
        ]
        joined = [
            jnp.concatenate([ups[0][0], ups[1][0]], axis=1),
            jnp.concatenate(downs, axis=0),
            jnp.concatenate([ups[0][1], ups[1][1]], axis=1),
            jnp.concatenate([ups[0][2], ups[1][2]], axis=0),
        ]
        up_grad_t, down_grad_t, up_grad_l, down_grad_l = (
            lax.psum(lax.psum_scatter(g, "tensor", scatter_dimension=axis, tiled=True), "dp")
            for g, axis in zip(joined, (1, 0, 1, 0))
        )
        rows = grads.shape[0] // 2
        joint_t, mix_t, joint_l, mix_l, norm_t, norm_l = lax.psum(open_up(
            open_half_kernel, 4, 2, [(wt, 3 * wt), (wt, wt), (wl, 3 * wl), (wl, wl), (4, wt), (4, wl)],
            [(wt, wt)] * 4 + [(256, wt)], sides, [],
            parts(grads, FIELDS_HALF) + parts(grads, FIELDS_HALF, rows),
        ), AXES)
    return (
        result_t[None],
        result_l.T[None],
        dtext[None],
        dlayout.T[None],
        joint_t,
        mix_t,
        norm_t,
        up_grad_t.astype(F32),
        down_grad_t.astype(F32),
        joint_l,
        mix_l,
        norm_l,
        up_grad_l.astype(F32),
        down_grad_l.astype(F32),
    )


def solution(mesh):
    many = (mesh.shape["dp"], mesh.shape["tensor"])
    pages = P(("dp", "tensor"), None, None)
    columns, rows = P(None, "tensor"), P("tensor", None)
    return jax.shard_map(
        functools.partial(shards, many),
        mesh=mesh,
        in_specs=(
            pages, pages, P(("dp", "tensor")), P(), P(), P(), columns, rows, P(), P(), P(), columns, rows, pages, pages,
        ),
        out_specs=(
            pages, pages, pages, pages, P(), P(), P(), columns, rows, P(), P(), P(), columns, rows,
        ),
        check_vma=False,
    )
```

```python
import functools
import math

import jax
import jax.numpy as jnp
from jax import lax
from jax.experimental import pallas as pl
from jax.experimental.pallas import tpu as pltpu
from jax.sharding import PartitionSpec as P

HEADS = 12
NEG_FILL = -1e30
EPS = 1e-05
F32 = jnp.float32
BF16 = jnp.bfloat16
VMEM_SPEC = pl.BlockSpec(memory_space=pltpu.VMEM)
SMEM_SPEC = pl.BlockSpec(memory_space=pltpu.SMEM)
SCALE = 1.0


def nn(left, right):
    return lax.dot_general(left, right, (((1,), (0,)), ((), ())), preferred_element_type=F32)


def nt(left, right):
    return lax.dot_general(left, right, (((1,), (1,)), ((), ())), preferred_element_type=F32)


def tn(left, right):
    return lax.dot_general(left, right, (((0,), (0,)), ((), ())), preferred_element_type=F32)


def gelu_pair(hidden):
    below = 0.5 * (1.0 + lax.erf(hidden * math.sqrt(0.5)))
    bell = jnp.exp(-0.5 * hidden * hidden)
    return hidden * below, below + hidden * bell * (1.0 / math.sqrt(2.0 * math.pi))


def unit(hidden):
    center = hidden - jnp.mean(hidden, axis=-1, keepdims=True)
    spread = jnp.mean(center * center, axis=-1, keepdims=True)
    rate = lax.rsqrt(spread + EPS)
    return center * rate, rate


def unit_back(normed, rate, grad, gain):
    scaled = grad * gain
    return rate * (
        scaled
        - jnp.mean(scaled, axis=-1, keepdims=True)
        - normed * jnp.mean(scaled * normed, axis=-1, keepdims=True)
    )


def lane_masks(head, lane):
    base = (head // 8) * 8
    return (lane // 64) == (head % 2), (lane // 16) == (head - base)


ORDERS = (((0, 2, 1, 3), (1, 0, 2, 3)), ((1, 2, 0, 3), (2, 0, 1, 3)), ((0, 2, 1, 3), (2, 0, 1, 3)), ((0, 1, 2, 3), (1, 0, 2, 3)))
FIELDS_DOWN = ((("down", 0, 192),),)
FIELDS_UP = ((("left", 0, 96), ("right", 0, 96), ("low", 0, 32)),)
FIELDS_HALF = (
    (("query", 0, 32), ("key", 0, 32), ("value", 0, 16), ("mix", 0, 16), ("low", 0, 16)),
    (("query", 256, 16), ("key", 256, 16), ("value", 128, 32), ("mix", 128, 32)),
)
PLANS = (FIELDS_DOWN, FIELDS_UP, FIELDS_HALF)
HALF_ROWS = {"query": 384, "key": 384, "value": 384, "mix": 384, "low": 128}
EVENTS = (
    "B2", "D.core", "B3", "U.core", "turn", "p0", "p1", "D0.0", "U0.0", "close", "in", "D0.1", "A.core",
    "U0.1", "D0.2", "U0.2", "A0.0", "A1.0", "D0.3", "A1.1", "A0.1", "U0.3", "A1.2", "A0.2", "U0.4", "D0.4",
    "A1.3", "A0.3", "A1.4", "A0.4", "A1.5", "U0.5", "D0.5", "A0.5", "D0.6", "oD", "A1.6", "A0.6", "U0.6",
    "oU",
)


def leaf_of(fields):
    return sum(n for _, _, n in fields)


def streams_of(plan):
    base = 0
    first = sum(len(p) for p in PLANS[:PLANS.index(plan)])
    for i, fields in enumerate(plan):
        yield first + i, base, leaf_of(fields), fields
        base += 8 * leaf_of(fields)


def rows_of(plan):
    return sum(8 * leaf_of(fields) for fields in plan)


def sides_of(dp, tensor):
    bits = [(dp >> b) & 1 for b in range(4)]
    values = [tensor & 1]
    for orders in ORDERS:
        values += [bits[o[0]] * 4 + bits[o[1]] * 2 + bits[o[2]] for o in orders]
    return jnp.stack(values)


def place(out, sides, core, plan, field, value, start=0, shift=0, skip=0):
    for number, base, leaf, fields in streams_of(plan):
        mask = sides[1 + 2 * number + core]
        inner = 0
        for name, first, n in fields:
            if name == field:
                for l in range(8):
                    at = first + l * n - start
                    if 0 <= at < value.shape[0]:
                        row = shift + base + inner + n * skip + leaf * jnp.bitwise_xor(mask, l)
                        row = pl.multiple_of(row, math.gcd(math.gcd(base + inner, leaf), 16))
                        out[pl.ds(row, n), :] = value[at:at + n, :]
            inner += n


def place_half(out, sides, field, value, skip=0):
    half = HALF_ROWS[field]
    for core in range(2):
        shift = jnp.bitwise_xor(sides[0], core) * rows_of(FIELDS_HALF)
        place(out, sides, core, FIELDS_HALF, field, value[core * half:(core + 1) * half, :], 0, shift, skip)


def fetch(pairs, sems):
    copies = [pltpu.make_async_copy(src, dst, sems.at[i]) for i, (src, dst) in enumerate(pairs)]
    for copy in copies:
        copy.start()
    return copies


def front_kernel(
    count_ref, sides, text_any, layout_any, joint_t_any, joint_l_any, mix_t_any, mix_l_any,
    qkv_t, qkv_l, mixed_t, mixed_l, normed_t, normed_l, stats,
    text_ref, layout_ref, joint_t, joint_l, mix_t, mix_l, mix_acc, flipped, sems,
):
    slots, width_t = text_ref.shape
    width_l = layout_ref.shape[1]
    columns = [slice(j * width_t, (j + 1) * width_t) for j in range(3)]
    copies = fetch(
        [
            (layout_any.at[0], flipped), (joint_l_any, joint_l), (text_any.at[0], text_ref),
            *((joint_t_any.at[:, c], joint_t.at[:, c]) for c in columns),
            (mix_t_any, mix_t), (mix_l_any, mix_l),
        ],
        sems,
    )
    count = count_ref[0]
    mix_acc[...] = jnp.zeros_like(mix_acc)
    stats[...] = jnp.zeros_like(stats)
    copies[0].wait()
    copies[1].wait()
    layout_ref[...] = flipped[...].T
    for j in range(3):
        qkv_l[:, j * 256:j * 256 + width_l] = nn(
            layout_ref[...], joint_l[:, j * width_l:(j + 1) * width_l]
        ).astype(BF16)
        qkv_l[:, j * 256 + width_l:(j + 1) * 256] = jnp.zeros((slots, 256 - width_l), BF16)
    copies[2].wait()

    def project(j, carry):
        c = pl.ds(pl.multiple_of(j * width_t, width_t), width_t)
        pltpu.make_async_copy(joint_t_any.at[:, c], joint_t.at[:, c], sems.at[3 + j]).wait()
        qkv_t[:, c] = nn(text_ref[...], joint_t[:, c]).astype(BF16)
        return carry

    lax.fori_loop(0, 3, project, 0)
    lane = lax.broadcasted_iota(jnp.int32, (slots, 128), 1)
    dead = lax.broadcasted_iota(jnp.int32, (slots, slots), 1) >= count

    def pair_step(pair, carry):
        spot = lambda start: pl.ds(pl.multiple_of(start, 128), 128)
        at_l = (pair // 4) * 128
        query_t, key_t, value_t = (qkv_t[:, spot(j * width_t + pair * 128)] for j in range(3))
        query_l, key_l, value_l = (qkv_l[:, spot(j * 256 + at_l)] for j in range(3))
        keys = jnp.concatenate([key_t, key_l], axis=1)
        values = jnp.concatenate([value_t, value_l], axis=1)
        masks = [lane_masks(2 * pair + side, lane) for side in range(2)]
        logits = []
        for mask_t, mask_l in masks:
            queries = jnp.concatenate(
                [
                    jnp.where(mask_t, query_t * 0.125, 0),
                    jnp.where(mask_l, query_l * 0.25, 0),
                ],
                axis=1,
            ).astype(BF16)
            logits.append(jnp.where(dead, NEG_FILL, nt(queries, keys)))
        outs = []
        for side in range(2):
            top = jnp.max(logits[side], axis=1, keepdims=True)
            raised = jnp.exp(logits[side] - top)
            mass = jnp.sum(raised, axis=1, keepdims=True)
            stats[...] = jnp.where(lane == 2 * pair + side, top + jnp.log(mass), stats[...])
            outs.append(nn(raised.astype(BF16), values) * (1.0 / mass))
        mixed_t[:, spot(pair * 128)] = jnp.where(masks[1][0], outs[1][:, :128], outs[0][:, :128]).astype(BF16)
        mix_acc[:, spot(at_l)] = (
            mix_acc[:, spot(at_l)]
            + jnp.where(masks[0][1], outs[0][:, 128:], 0.0)
            + jnp.where(masks[1][1], outs[1][:, 128:], 0.0)
        )
        return carry

    lax.fori_loop(0, HEADS // 2, pair_step, 0)
    mixed_l[...] = mix_acc[:, :width_l].astype(BF16)
    copies[6].wait()
    normed, rate = unit(text_ref[...].astype(F32) + nn(mixed_t[...], mix_t[...]))
    normed_t[...] = normed
    stats[...] = jnp.where(lane == 16, rate, stats[...])
    copies[7].wait()
    normed, rate = unit(layout_ref[...].astype(F32) + nn(mixed_l[...], mix_l[...]))
    normed_l[...] = normed
    stats[...] = jnp.where(lane == 17, rate, stats[...])


def column(stats, lane, which):
    return jnp.sum(jnp.where(lane == which, stats[...], 0.0), axis=1, keepdims=True)


ANY_SPEC = pl.BlockSpec(memory_space=pltpu.HBM)


def call(kernel, micros, outs, args, scratch=(), specs=None, aliases=None, limit=8, out_specs=None):
    moved = sum(math.prod(a.shape) * a.dtype.itemsize for a in args)
    return pl.pallas_call(
        kernel,
        out_shape=[(pltpu.VMEM(s, d) if kept else jax.ShapeDtypeStruct(s, d)) for s, d, kept in outs],
        in_specs=specs or [VMEM_SPEC] * len(args),
        out_specs=out_specs or [VMEM_SPEC] * len(outs),
        scratch_shapes=list(scratch),
        input_output_aliases=aliases or {},
        compiler_params=pltpu.CompilerParams(vmem_limit_bytes=limit * 1024 * 1024),
        cost_estimate=pl.CostEstimate(flops=int(micros * SCALE * 1.1e9), bytes_accessed=moved, transcendentals=0),
    )(*args)


def front(count, sides, text, layout, joint_t, joint_l, mix_t, mix_l):
    _, s, wt = text.shape
    wl = layout.shape[1]
    return call(
        front_kernel,
        12,
        [
            ((s, 3 * wt), BF16, True), ((s, 768), BF16, True), ((s, wt), BF16, True), ((s, wl), BF16, True),
            ((s, wt), F32, True), ((s, wl), F32, True), ((s, 128), F32, True),
        ],
        (count, sides, text, layout, joint_t, joint_l, mix_t, mix_l),
        [
            pltpu.VMEM((s, wt), BF16), pltpu.VMEM((s, wl), BF16), pltpu.VMEM((wt, 3 * wt), BF16),
            pltpu.VMEM((wl, 3 * wl), BF16), pltpu.VMEM((wt, wt), BF16), pltpu.VMEM((wl, wl), BF16),
            pltpu.VMEM((s, 256), F32), pltpu.VMEM((wl, s), BF16), pltpu.SemaphoreType.DMA((8,)),
        ],
        [SMEM_SPEC] * 2 + [ANY_SPEC] * 6,
        limit=48,
    )


def feed_kernel(
    sides, normed_t, normed_l, norms_t, norms_l, *refs,
):
    far_refs, refs = refs[:10], refs[10:]
    (
        result_t, result_l, second_t, second_l, dfeed_t, dfeed_l, low_t, low_l,
        act_t0, act_t1, slope_t0, slope_t1, act_l0, act_l1, slope_l0, slope_l1,
        dnorm_t, dnorm_l, down_far,
    ) = refs[:19]
    cot_t, cot_l, up_t0, up_t1, down_t0, down_t1, up_l0, up_l1, down_l0, down_l1 = far_refs
    step = 512
    cuts = [slice(at, at + step) for at in range(0, up_t0.shape[1], step)]
    first_t = normed_t[...] * norms_t[0:1, :] + norms_t[1:2, :]
    low_t[...] = first_t.astype(BF16)
    first_l = normed_l[...] * norms_l[0:1, :] + norms_l[1:2, :]
    low_l[...] = first_l.astype(BF16)
    for up, act, slope in ((up_t0, act_t0, slope_t0), (up_t1, act_t1, slope_t1)):
        for cut in cuts:
            active, rise = gelu_pair(nn(low_t[...], up[:, cut]))
            act[:, cut] = active.astype(BF16)
            slope[:, cut] = rise.astype(BF16)
    for up, act, slope in ((up_l0, act_l0, slope_l0), (up_l1, act_l1, slope_l1)):
        active, rise = gelu_pair(nn(low_l[...], up[...]))
        act[...] = active.astype(BF16)
        slope[...] = rise.astype(BF16)
    summed_l = first_l + nt(act_l0[...], down_l0[...]) + nt(act_l1[...], down_l1[...])
    summed_t = normed_t[...] * norms_t[0:1, :] + norms_t[1:2, :] + (
        nn(act_t0[...], down_t0[...]) + nn(act_t1[...], down_t1[...])
    )
    for summed, norms, cot, result, second, dfeed, dnorm in (
        (summed_t, norms_t, cot_t, result_t, second_t, dfeed_t, dnorm_t),
        (summed_l, norms_l, cot_l, result_l, second_l, dfeed_l, dnorm_l),
    ):
        normed, rate = unit(summed)
        value = (normed * norms[2:3, :] + norms[3:4, :]).astype(BF16)
        result[...] = value if result is result_t else value.T
        grad = (cot[0] if cot is cot_t else cot[0].T).astype(F32)
        dnorm[0:1, :] = jnp.sum(grad * normed, axis=0, keepdims=True)
        dnorm[1:2, :] = jnp.sum(grad, axis=0, keepdims=True)
        back = unit_back(normed, rate, grad, norms[2:3, :])
        second[...] = back
        dfeed[...] = back.astype(BF16)
    down_kernel(sides, 1, act_t1, dfeed_t, down_far)


def feed(sides, normed_t, normed_l, norms_t, norms_l, cot_t, cot_l, weights):
    s, wt = normed_t.shape
    wl = normed_l.shape[1]
    ht, hl = weights[0].shape[1], weights[4].shape[1]
    return call(
        feed_kernel,
        16,
        [((s, wt), BF16, False), ((wl, s), BF16, False)]
        + [((s, wt), F32, True), ((s, wl), F32, True)]
        + [((s, wt), BF16, True), ((s, wl), BF16, True)] * 2
        + [((s, ht), BF16, True)] * 4
        + [((s, hl), BF16, True)] * 4
        + [((2, wt), F32, True), ((2, wl), F32, True), ((ht, wt), BF16, False)],
        (sides, normed_t, normed_l, norms_t, norms_l, cot_t, cot_l) + tuple(weights),
        specs=[SMEM_SPEC] + [VMEM_SPEC] * 14,
        limit=13,
    )


def down_kernel(sides, far, act, dfeed, out):
    core = jnp.bitwise_xor(sides[0], far)
    (number, _, leaf, _), = streams_of(FIELDS_DOWN)
    mask = sides[1 + 2 * number + core]

    def chunk(c, carry):
        at = pl.ds(pl.multiple_of(c * 4 * leaf, 4 * leaf), 4 * leaf)
        value = tn(act[:, at], dfeed[...]).astype(BF16)
        for i in range(4):
            row = leaf * jnp.bitwise_xor(mask, 4 * c + i)
            out[pl.ds(pl.multiple_of(row, 16), leaf), :] = value[i * leaf:(i + 1) * leaf, :]
        return carry

    lax.fori_loop(0, 2, chunk, 0)


def up_body(
    sides, far, dfeed_t, dfeed_l, low_t, low_l, down_t, down_l, slope_t, slope_l, act_l, up_t, up_l, prev_t, prev_l,
    grads, dfirst_t, dfirst_l, dhid,
):
    wt = low_t.shape[1]
    wl = low_l.shape[1]
    core = jnp.bitwise_xor(sides[0], far)
    (number, _, leaf, fields), = streams_of(FIELDS_UP)
    mask = sides[1 + 2 * number + core]
    part = fields[0][2]

    def chunk(c, carry):
        at = pl.ds(pl.multiple_of(c * wt, wt), wt)
        dhid[:, at] = (nt(dfeed_t[...], down_t[at, :]) * slope_t[:, at].astype(F32)).astype(BF16)
        value = tn(low_t[...], dhid[:, at]).astype(BF16)
        for l in range(8):
            row = leaf * jnp.bitwise_xor(mask, l) + part * c
            grads[pl.ds(pl.multiple_of(row, 16), part), :] = value[l * part:(l + 1) * part, :]
        return carry

    lax.fori_loop(0, down_t.shape[0] // wt, chunk, 0)
    dfirst_t[...] = prev_t[...] + nt(dhid[...], up_t[...])
    hl = down_l.shape[1]
    dhidden = (nn(dfeed_l[...], down_l[...]) * slope_l[...].astype(F32)).astype(BF16)
    lower = tn(act_l[...], dfeed_l[...]).astype(BF16)
    packed = jnp.concatenate([tn(low_l[...], dhidden).astype(BF16), lower[:wl, :], lower[wl:, :]], axis=1)
    place(grads, sides, core, FIELDS_UP, "low", jnp.concatenate([packed, jnp.zeros((64, wt), BF16)], axis=0))
    dfirst_l[...] = prev_l[...] + nt(dhidden, up_l[...])


def up_kernel(sides, *refs):
    up_body(sides, 0, *refs)


def up_down_kernel(*refs):
    sides, act_t, refs = refs[0], refs[1], refs[2:]
    down_kernel(sides, 0, act_t, refs[0], refs[13])
    up_body(sides, 1, *refs[:13], *refs[14:])


def up_grad(sides, act_t, *args):
    dfeed_t, dfeed_l, low_t, low_l, down_t = args[:5]
    s, wt = low_t.shape
    wl = low_l.shape[1]
    ht = down_t.shape[0]
    outs = [((ht + wl + 64, wt), BF16, False), ((s, wt), F32, True), ((s, wl), F32, True)]
    scratch = [pltpu.VMEM((s, ht), BF16)]
    if act_t is None:
        specs = [SMEM_SPEC] + [VMEM_SPEC] * len(args)
        return call(up_kernel, 5, outs, (sides,) + args, scratch, specs)
    specs = [SMEM_SPEC] + [VMEM_SPEC] * (len(args) + 1)
    return call(up_down_kernel, 8, [((ht, wt), BF16, False)] + outs, (sides, act_t) + args, scratch, specs)


def turn_kernel(
    sides, mixed_t, mixed_l, normed_t, normed_l, stats, dfirst_t, dfirst_l, norms_t, norms_l, dnorm_t, dnorm_l, mix_t, mix_l,
    grads, dtext, dlayout, dmix_t, dmix_l, mix_low, norm_low, djoint_t, acc_l,
):
    slots, wt = mixed_t.shape
    wl = mixed_l.shape[1]
    acc_l[...] = jnp.zeros_like(acc_l)
    djoint_t[...] = jnp.zeros_like(djoint_t)
    lane = lax.broadcasted_iota(jnp.int32, (slots, 128), 1)
    kept = []
    for n, (first, normed, norms, dnorm, width, mixed, mix, dmix) in enumerate((
        (dfirst_t, normed_t, norms_t, dnorm_t, wt, mixed_t, mix_t, dmix_t),
        (dfirst_l, normed_l, norms_l, dnorm_l, wl, mixed_l, mix_l, dmix_l),
    )):
        grad = first[...]
        unitv = normed[...]
        gain_grad = jnp.sum(grad * unitv, axis=0, keepdims=True)
        shift_grad = jnp.sum(grad, axis=0, keepdims=True)
        rows = jnp.concatenate([gain_grad, shift_grad, dnorm[0:2, :]], axis=0)
        kept.append(jnp.concatenate(
            [rows.astype(BF16), jnp.zeros((12, width), BF16)], axis=0
        ) if width == wt else jnp.concatenate(
            [jnp.concatenate([rows.astype(BF16), jnp.zeros((4, wt - width), BF16)], axis=1), jnp.zeros((44, wt), BF16)],
            axis=0,
        ))
        resid = unit_back(unitv, column(stats, lane, 16 + n), grad, norms[0:1, :])
        low = resid.astype(BF16)
        if n == 0:
            dtext[...] = resid
            place_half(grads, sides, "mix", tn(mixed[...], low).astype(BF16))
            dmix[...] = nt(low, mix[...]).astype(BF16)
        else:
            dlayout[...] = resid
            mix_low[...] = tn(mixed[...], low).astype(BF16)
            dmix[:, :wl] = nt(low, mix[...]).astype(BF16)
            dmix[:, wl:] = jnp.zeros((slots, 256 - wl), BF16)
    norm_low[...] = jnp.concatenate(kept, axis=0)


def turn(*args):
    s, wt = args[1].shape
    wl = args[2].shape[1]
    rows = 4 * wt + wl + 64
    return call(
        turn_kernel,
        4,
        [
            ((rows, wt), BF16, True), ((s, wt), F32, True), ((s, wl), F32, True), ((s, wt), BF16, True),
            ((s, 256), BF16, True), ((wl, wl), BF16, True), ((64, wt), BF16, True), ((s, 3 * wt), BF16, True),
            ((s, 768), F32, True),
        ],
        args,
        specs=[SMEM_SPEC] + [VMEM_SPEC] * (len(args) - 1),
    )


def pairs_kernel(span_ref, count_ref, qkv_t, qkv_l, stats, dmix_t, dmix_l, djoint_in, acc_in, djoint_t, acc_l):
    slots, wt = dmix_t.shape
    count = count_ref[0]
    lane = lax.broadcasted_iota(jnp.int32, (slots, 128), 1)
    dead = lax.broadcasted_iota(jnp.int32, (slots, slots), 1) >= count

    def pair_step(pair, carry):
        spot = lambda start: pl.ds(pl.multiple_of(start, 128), 128)
        at_l = (pair // 4) * 128
        query_t, key_t, value_t = (qkv_t[:, spot(j * wt + pair * 128)] for j in range(3))
        query_l, key_l, value_l = (qkv_l[:, spot(j * 256 + at_l)] for j in range(3))
        upper_t = dmix_t[:, spot(pair * 128)]
        upper_l = dmix_l[:, spot(at_l)]
        keys = jnp.concatenate([key_t, key_l], axis=1)
        values = jnp.concatenate([value_t, value_l], axis=1)
        kept = None
        for side in range(2):
            head = 2 * pair + side
            mask_t, mask_l = lane_masks(head, lane)
            queries = jnp.concatenate(
                [
                    jnp.where(mask_t, query_t * 0.125, 0),
                    jnp.where(mask_l, query_l * 0.25, 0),
                ],
                axis=1,
            ).astype(BF16)
            logits = jnp.where(dead, NEG_FILL, nt(queries, keys))
            probs = jnp.exp(logits - column(stats, lane, head))
            own_t = jnp.where(mask_t, upper_t, 0).astype(BF16)
            own_l = jnp.where(mask_l, upper_l, 0).astype(BF16)
            grad_t = nt(own_t, value_t)
            grad_s = nt(jnp.concatenate([own_t, own_l], axis=1), values)
            score_t = (probs * (grad_t - jnp.sum(grad_t * probs, axis=1, keepdims=True))).astype(BF16)
            score_l = (probs * (grad_s - jnp.sum(grad_s * probs, axis=1, keepdims=True))).astype(BF16)
            dvalue = tn(probs.astype(BF16), jnp.concatenate([upper_t, upper_l], axis=1))
            dquery_t = nn(score_t, key_t) * 0.125
            dkey_t = tn(score_t, query_t) * 0.125
            dquery_l = nn(score_l, key_l) * 0.25
            dkey_l = tn(score_l, query_l) * 0.25
            if side == 0:
                kept = (dquery_t, dkey_t, dvalue[:, :128])
            else:
                for j, (old, new) in enumerate(zip(kept, (dquery_t, dkey_t, dvalue[:, :128]))):
                    djoint_t[:, spot(j * wt + pair * 128)] = jnp.where(mask_t, new, old).astype(BF16)
            for j, part in enumerate((dquery_l, dkey_l, dvalue[:, 128:])):
                at = spot(j * 256 + at_l)
                acc_l[:, at] = acc_l[:, at] + jnp.where(mask_l, part, 0.0)
        return carry

    lax.fori_loop(span_ref[0], span_ref[1], pair_step, 0)


def pairs(lo, hi, prev, *args):
    s, wt = args[4].shape
    span = jnp.array([lo, hi], jnp.int32)
    return call(
        pairs_kernel,
        3 * (hi - lo),
        [((s, 3 * wt), BF16, True), ((s, 768), F32, True)],
        (span,) + args + tuple(prev),
        specs=[SMEM_SPEC] * 2 + [VMEM_SPEC] * 7,
        aliases={7: 0, 8: 1},
    )


def close_kernel(
    sides, text_ref, layout_ref, djoint_t, acc_l, mix_low, norm_low, part_ref,
    grads, djoint_l,
):
    wt = text_ref.shape[2]
    wl = layout_ref.shape[1]
    def block(j, carry):
        value = tn(text_ref[0], djoint_t[:, pl.ds(pl.multiple_of(j * wt, wt), wt)]).astype(BF16)
        place_half(grads, sides, "query", value, j)
        return carry

    lax.fori_loop(0, 2, block, 0)
    place_half(grads, sides, "value", tn(text_ref[0], djoint_t[:, 2 * wt:]).astype(BF16))
    for j in range(3):
        djoint_l[:, j * wl:(j + 1) * wl] = acc_l[:, j * 256:j * 256 + wl].astype(BF16)
    low = jnp.concatenate([nn(layout_ref[0], djoint_l[...]).astype(BF16), mix_low[...]], axis=1)
    place_half(grads, sides, "low", jnp.concatenate([low, norm_low[...]], axis=0))


def close(*args):
    text, layout = args[1:3]
    _, s, wt = text.shape
    wl = layout.shape[1]
    return call(
        close_kernel,
        3,
        [(args[7].shape, BF16, True), ((s, 3 * wl), BF16, True)],
        args,
        specs=[SMEM_SPEC] + [VMEM_SPEC] * (len(args) - 1),
        aliases={7: 0},
    )


def inputs_kernel(djoint_t, djoint_l, joint_t, joint_l, dtext_in, dlayout_in, dtext, dlayout):
    dtext[...] = dtext_in[...] + nt(djoint_t[...], joint_t[...])
    dlayout[...] = (dlayout_in[...] + nt(djoint_l[...], joint_l[...])).T


def input_grads(*args):
    s, wt = args[4].shape
    wl = args[5].shape[1]
    return call(inputs_kernel, 3, [((s, wt), F32, False), ((wl, s), F32, False)], args)


AXES = ("dp", "tensor")


def swap(value, bits, many):
    dp, tensor = many
    pairs = []
    for d in range(dp):
        for t in range(tensor):
            to = (d, t ^ 1) if bits == -1 else (d ^ (1 << bits[t]), t)
            pairs.append((d * tensor + t, to[0] * tensor + to[1]))
    return lax.ppermute(value, AXES, pairs)


def cut_of(value, base, rows):
    return lax.slice_in_dim(value, base, base + rows, axis=0)


def tie(values, *others):
    got = lax.optimization_barrier((tuple(values), tuple(others)))
    return got[0]


class Stream:
    def __init__(self, fields, orders, many):
        self.half, self.orders, self.many = 4 * leaf_of(fields), orders, many

    def launch(self, phase, value):
        bits = tuple(order[min(phase, 6 - phase)] for order in self.orders)
        self.flying = swap(value, bits, self.many)
        return [value]

    def begin(self, own, got, base):
        half = self.half
        self.keep = cut_of(own, base, half) + cut_of(got, base, half)
        return self.launch(0, cut_of(own, base + half, half) + cut_of(got, base + half, half))

    def finish(self, phase, token):
        got, = tie([self.flying], *token)
        keep = self.keep
        if phase < 2:
            half = keep.shape[0] // 2
            self.keep = cut_of(keep, 0, half) + cut_of(got, 0, half)
            return self.launch(phase + 1, cut_of(keep, half, half) + cut_of(got, half, half))
        if phase == 6:
            self.keep = (keep, got)
            return [got]
        self.keep = keep + got if phase < 4 else jnp.concatenate([keep, got], axis=0)
        return self.launch(phase + 1, self.keep)


def unplace(parts, sides, core, plan, field, out, half=0, which=(0, 1)):
    runs = []
    for i, (number, _, leaf, fields) in enumerate(streams_of(plan)):
        mask = sides[1 + 2 * number + core]
        inner = 0
        for name, first, n in fields:
            if name == field:
                for side in which:
                    part = parts[2 * i + side]

                    def copy(r, carry, first=first, n=n, inner=inner, part=part, mask=mask, side=side, leaf=leaf):
                        row = core * half + first + n * jnp.bitwise_xor(mask, 4 * side + r)
                        source = pl.ds(pl.multiple_of(inner + r * leaf, 16), n)
                        out[pl.ds(pl.multiple_of(row, 16), n), :] = part[source, :].astype(F32)
                        return carry

                    lax.fori_loop(0, 4, copy, 0)
                    start = core * half + first + 4 * n * jnp.bitwise_xor(mask // 4, side)
                    runs.append(pl.ds(pl.multiple_of(start, 4 * n), 4 * n))
            inner += n
    return runs


def stage(refs, sems, fill):
    flying = []
    for i, (field, out, columns, buffer) in enumerate(refs):
        fill(field, buffer)
        copy = pltpu.make_async_copy(buffer, out.at[:, columns], sems.at[i])
        copy.start()
        flying.append(copy)
    return flying


def open_down_kernel(sides, *refs):
    parts, (out, buffer, sems) = refs[:-3], refs[-3:]
    unplace(parts, sides, sides[0], FIELDS_DOWN, "down", buffer)
    copy = pltpu.make_async_copy(buffer, out, sems.at[0])
    copy.start()
    copy.wait()


def open_up_kernel(sides, *refs):
    parts, (up_t, up_l, down_l, left, right, low, sems) = refs[:-7], refs[-7:]
    wt = up_t.shape[0]
    wl, hl = up_l.shape
    fill = functools.partial(unplace, parts, sides, sides[0], FIELDS_UP)
    flying = stage(
        [("left", up_t, slice(0, wt), left), ("right", up_t, slice(wt, 2 * wt), right)], sems, fill
    )
    fill("low", low)
    up_l[...] = low[:wl, :hl]
    down_l[:, :wl] = low[:wl, hl:hl + wl].T
    down_l[:, wl:] = low[:wl, hl + wl:].T
    for copy in flying:
        copy.wait()


def send_half(own, other, sides, outs, which, sems):
    flying = []
    for field, out, columns, buffer in outs:
        for parts, core in ((own, sides[0]), (other, 1 - sides[0])):
            for run in unplace(parts, sides, core, FIELDS_HALF, field, buffer, HALF_ROWS[field], (which,)):
                copy = pltpu.make_async_copy(buffer.at[run, :], out.at[run, columns], sems.at[len(flying)])
                copy.start()
                flying.append(copy)
    return flying


def half_outs(joint_t, mix_t, buffers):
    wt = mix_t.shape[0]
    names = ("query", "key", "value", "mix")
    places = [(joint_t, slice(j * wt, (j + 1) * wt)) for j in range(3)] + [(mix_t, slice(0, wt))]
    return [(name, *there, buffer) for name, there, buffer in zip(names, places, buffers)]


def first_half_kernel(sides, *refs):
    count = len(FIELDS_HALF)
    spread = lambda refs: [ref for ref in refs for _ in range(2)]
    own, other = spread(refs[:count]), spread(refs[count:2 * count])
    joint_t, mix_t, mark, *buffers, sems = refs[2 * count:]
    mark[...] = jnp.zeros_like(mark)
    for copy in send_half(own, other, sides, half_outs(joint_t, mix_t, buffers), 0, sems):
        copy.wait()


def open_half_kernel(sides, *refs):
    count = 2 * len(FIELDS_HALF)
    own, other, refs = refs[:count], refs[count:2 * count], refs[2 * count + 2:]
    joint_t, mix_t, joint_l, mix_l, norm_t, norm_l, *buffers, low, sems = refs
    wl = mix_l.shape[0]
    flying = send_half(own, other, sides, half_outs(joint_t, mix_t, buffers), 1, sems)
    for parts, core in ((own, sides[0]), (other, 1 - sides[0])):
        unplace(parts, sides, core, FIELDS_HALF, "low", low, HALF_ROWS["low"])
    joint_l[...] = low[:wl, :3 * wl]
    mix_l[...] = low[:wl, 3 * wl:]
    norm_t[...] = low[wl:wl + 4, :]
    norm_l[...] = low[wl + 16:wl + 20, :wl]
    for copy in flying:
        copy.wait()


def open_half(sides, own_parts, to_far, wt, wl):
    buffers = [pltpu.VMEM((wt, wt), F32)] * 4
    sems = pltpu.SemaphoreType.DMA((4 * len(own_parts),))
    big = [((wt, 3 * wt), F32, False), ((wt, wt), F32, False)]
    keeps, gots = own_parts[0::2], own_parts[1::2]
    far_keeps = to_far(keeps, 0)
    *begun, mark = call(
        first_half_kernel, 3, big + [((8, 128), F32, False)], (sides, *keeps, *far_keeps), buffers + [sems],
        [SMEM_SPEC] + [VMEM_SPEC] * 2 * len(keeps), limit=24, out_specs=[ANY_SPEC] * 2 + [VMEM_SPEC],
    )
    gots = [tie([got], mark)[0] for got in gots]
    both = lambda one, two: [part for pair in zip(one, two) for part in pair]
    args = (sides, *both(keeps, gots), *both(far_keeps, to_far(gots, 1)), *begun)
    return call(
        open_half_kernel, 3,
        big + [(shape, F32, False) for shape in ((wl, 3 * wl), (wl, wl), (4, wt), (4, wl))],
        args, buffers + [pltpu.VMEM((256, wt), F32), sems],
        [SMEM_SPEC] + [VMEM_SPEC] * (len(args) - 3) + [ANY_SPEC] * 2,
        aliases={len(args) - 2: 0, len(args) - 1: 1}, limit=24,
        out_specs=[ANY_SPEC] * 2 + [VMEM_SPEC] * 4,
    )


def open_up(kernel, micros, direct, outs, buffers, sides, token, parts):
    if token:
        parts = [tie([parts[0]], *token)[0], *parts[1:]]
    return call(
        kernel, micros, [(shape, F32, False) for shape in outs], (sides,) + tuple(parts),
        [pltpu.VMEM(shape, F32) for shape in buffers] + [pltpu.SemaphoreType.DMA((4,))],
        [SMEM_SPEC] + [VMEM_SPEC] * len(parts), limit=24,
        out_specs=[ANY_SPEC] * direct + [VMEM_SPEC] * (len(outs) - direct),
    )


def shards(
    many, text_input, layout_input, page_counts, text_joint, text_mixing, text_norms, text_upward, text_downward,
    layout_joint, layout_mixing, layout_norms, layout_upward, layout_downward, text_cotangent, layout_cotangent,
):
    dp, tensor = many
    wt, wl = text_input.shape[2], layout_input.shape[2]
    layout_flip = layout_input.swapaxes(1, 2)
    halves = tensor == 2 and dp == 16
    own = (text_upward, text_downward, layout_upward, layout_downward.T)
    if halves:
        far = tuple(swap(w, -1, many) for w in own)
    else:
        whole = [
            lax.all_gather(w, "tensor", axis=axis, tiled=True) for w, axis in zip(own, (1, 0, 1, 1))
        ]
        cut = lambda w, axis, i: lax.slice_in_dim(w, i * (w.shape[axis] // 2), (i + 1) * (w.shape[axis] // 2), axis=axis)
        own = tuple(cut(w, axis, 0) for w, axis in zip(whole, (1, 0, 1, 1)))
        far = tuple(cut(w, axis, 1) for w, axis in zip(whole, (1, 0, 1, 1)))
    sides = sides_of(lax.axis_index("dp").astype(jnp.int32), lax.axis_index("tensor").astype(jnp.int32))
    if not halves:
        sides = jnp.zeros_like(sides)
    (
        qkv_t, qkv_l, mixed_t, mixed_l, normed_t, normed_l, stats,
    ) = front(page_counts, sides, text_input, layout_flip, text_joint, layout_joint, text_mixing, layout_mixing)
    up_t0, down_t0, up_l0, down_l0 = own
    up_t1, down_t1, up_l1, down_l1 = far
    (
        result_t, result_l, second_t, second_l, dfeed_t, dfeed_l, low_t, low_l,
        act_t0, act_t1, slope_t0, slope_t1, act_l0, act_l1, slope_l0, slope_l1, dnorm_t, dnorm_l, down_far,
    ) = feed(
        sides, normed_t, normed_l, text_norms, layout_norms, text_cotangent, layout_cotangent.swapaxes(1, 2),
        (own[0], far[0], own[1], far[1], own[2], far[2], own[3], far[3]),
    )
    run = {"token": [dfeed_t], "state": None, "first": (second_t, second_l)}
    streams = {
        "%s%d" % (name, number - first): Stream(fields, ORDERS[number], many)
        for name, plan in zip("DUA", PLANS)
        for first in [sum(len(p) for p in PLANS[:PLANS.index(plan)])]
        for number, _, _, fields in streams_of(plan)
    }
    got = {}
    if halves:
        got["D"] = swap(down_far, -1, many)

    def held(value):
        return tie([value], *run["token"])[0]

    def far_grads():
        down_own, up_far, *run["first"] = up_grad(
            sides, act_t0, held(dfeed_t),
            dfeed_l, low_t, low_l, down_t1, down_l1, slope_t1, slope_l1, act_l1, up_t1, up_l1, *run["first"]
        )
        run["down_own"], run["up_far"], run["token"] = down_own, up_far, [run["first"][0]]
        if halves:
            got["U"] = swap(up_far, -1, many)

    def own_grads():
        run["up_own"], *run["first"] = up_grad(
            sides, None, held(dfeed_t),
            dfeed_l, low_t, low_l, down_t0, down_l0, slope_t0, slope_l0, act_l0, up_t0, up_l0, *run["first"]
        )
        run["token"] = [run["first"][0]]

    def turn_back():
        run["grads"], run["dtext"], run["dlayout"], run["dmix_t"], run["dmix_l"], run["mix_low"], run["norm_low"], *run["state"] = turn(
            sides, mixed_t, mixed_l, normed_t, normed_l, stats, held(run["first"][0]), run["first"][1], text_norms,
            layout_norms, dnorm_t, dnorm_l, text_mixing, layout_mixing,
        )
        run["token"] = [run["dmix_t"]]

    def pair_grads(lo, hi):
        run["state"] = pairs(
            lo, hi, run["state"], page_counts, qkv_t, qkv_l, stats, held(run["dmix_t"]), run["dmix_l"]
        )
        run["token"] = [run["state"][1]]

    def close_up():
        state = run["state"]
        run["grads"], run["djoint_l"] = close(
            sides, text_input, layout_flip, state[0], held(state[1]), run["mix_low"], run["norm_low"], run["grads"],
        )
        run["token"] = [run["djoint_l"]]
        if halves:
            rows = run["grads"].shape[0] // 2
            run["half_own"] = cut_of(run["grads"], 0, rows)
            got["A"] = swap(cut_of(run["grads"], rows, rows), -1, many)

    def inputs_up():
        run["dtext"], run["dlayout"] = input_grads(
            run["state"][0], held(run["djoint_l"]), text_joint, layout_joint, run["dtext"], run["dlayout"]
        )
        run["token"] = [run["dlayout"]]

    ht, hl = text_upward.shape[1], layout_upward.shape[1]

    def parts_of(name, plan):
        return [part for i in range(len(plan)) for part in streams["%s%d" % (name, i)].keep]

    def open_down():
        run["down"], = open_up(open_down_kernel, 3, 1, [(ht, wt)], [(ht, wt)], sides, run["token"], parts_of("D", FIELDS_DOWN))
        run["token"] = [run["down"]]

    def open_upper():
        run["up"] = open_up(
            open_up_kernel, 3, 1, [(wt, ht), (wl, hl), (wl, hl)], [(wt, wt)] * 2 + [(256, wt)], sides, run["token"], parts_of("U", FIELDS_UP)
        )
        run["token"] = [run["up"][1]]

    kernels = {
        "B2": far_grads, "B3": own_grads, "turn": turn_back, "p0": lambda: pair_grads(0, 3),
        "p1": lambda: pair_grads(3, 6), "close": close_up, "in": inputs_up,
    }
    opens = {"oD": open_down, "oU": open_upper}
    owns = {"D": ("down_own", FIELDS_DOWN), "U": ("up_own", FIELDS_UP), "A": ("half_own", FIELDS_HALF)}
    for event in EVENTS if halves else [e for e in EVENTS if e in kernels]:
        if event in kernels:
            kernels[event]()
        elif event in opens:
            opens[event]()
        else:
            name, step = event.split(".")
            if step == "core":
                here, = tie([got[name]], *run["token"])
                own_of, plan = owns[name]
                run["token"], base = [], 0
                for i, fields in enumerate(plan):
                    run["token"] += streams["%s%d" % (name, i)].begin(run[own_of], here, base)
                    base += 8 * leaf_of(fields)
            else:
                run["token"] = streams[name].finish(int(step), run["token"])
    grads, dtext, dlayout = run["grads"], run["dtext"], run["dlayout"]
    down_own, up_own, up_far = run["down_own"], run["up_own"], run["up_far"]

    if halves:
        own_parts = parts_of("A", FIELDS_HALF)
        down_grad_t = run["down"]
        up_grad_t, up_grad_l, down_grad_l = run["up"]
        down_grad_l = down_grad_l.T
        joint_t, mix_t, joint_l, mix_l, norm_t, norm_l = open_half(
            sides, own_parts, lambda parts, side: [swap(part, -1, many) for part in parts], wt, wl
        )
    else:
        def parts(packed, plan, shift=0):
            return [
                cut_of(packed, shift + base + i * 4 * leaf, 4 * leaf)
                for _, base, leaf, _ in streams_of(plan) for i in range(2)
            ]

        hidden, wide = down_own.shape[0], up_l0.shape[1]
        downs = [
            open_up(open_down_kernel, 3, 1, [(hidden, wt)], [(hidden, wt)], sides, [], parts(p, FIELDS_DOWN))[0]
            for p in (down_own, down_far)
        ]
        ups = [
            open_up(
                open_up_kernel, 3, 1, [(wt, hidden), (wl, wide), (wl, wide)], [(wt, wt)] * 2 + [(256, wt)], sides, [],
                parts(p, FIELDS_UP),
            )
            for p in (up_own, up_far)
        ]
        joined = [
            jnp.concatenate([ups[0][0], ups[1][0]], axis=1),
            jnp.concatenate(downs, axis=0),
            jnp.concatenate([ups[0][1], ups[1][1]], axis=1),
            jnp.concatenate([ups[0][2].T, ups[1][2].T], axis=0),
        ]
        up_grad_t, down_grad_t, up_grad_l, down_grad_l = (
            lax.psum(lax.psum_scatter(g, "tensor", scatter_dimension=axis, tiled=True), "dp")
            for g, axis in zip(joined, (1, 0, 1, 0))
        )
        rows = grads.shape[0] // 2
        far_parts = parts(grads, FIELDS_HALF, rows)
        joint_t, mix_t, joint_l, mix_l, norm_t, norm_l = lax.psum(
            open_half(sides, parts(grads, FIELDS_HALF), lambda parts, side: far_parts[side::2], wt, wl), AXES
        )
    return (
        result_t[None],
        result_l.T[None],
        dtext[None],
        dlayout.T[None],
        joint_t,
        mix_t,
        norm_t,
        up_grad_t.astype(F32),
        down_grad_t.astype(F32),
        joint_l,
        mix_l,
        norm_l,
        up_grad_l.astype(F32),
        down_grad_l.astype(F32),
    )


def solution(mesh):
    many = (mesh.shape["dp"], mesh.shape["tensor"])
    pages = P(("dp", "tensor"), None, None)
    columns, rows = P(None, "tensor"), P("tensor", None)
    return jax.shard_map(
        functools.partial(shards, many),
        mesh=mesh,
        in_specs=(
            pages, pages, P(("dp", "tensor")), P(), P(), P(), columns, rows, P(), P(), P(), columns, rows, pages, pages,
        ),
        out_specs=(
            pages, pages, pages, pages, P(), P(), P(), columns, rows, P(), P(), P(), columns, rows,
        ),
        check_vma=False,
    )
```

```python
import functools
import math

import jax
import jax.numpy as jnp
from jax import lax
from jax.experimental import pallas as pl
from jax.experimental.pallas import tpu as pltpu
from jax.sharding import PartitionSpec as P

HEADS = 12
NEG_FILL = -1e30
EPS = 1e-05
F32 = jnp.float32
BF16 = jnp.bfloat16
VMEM_SPEC = pl.BlockSpec(memory_space=pltpu.VMEM)
SMEM_SPEC = pl.BlockSpec(memory_space=pltpu.SMEM)
SCALE = 1.0


def nn(left, right):
    return lax.dot_general(left, right, (((1,), (0,)), ((), ())), preferred_element_type=F32)


def nt(left, right):
    return lax.dot_general(left, right, (((1,), (1,)), ((), ())), preferred_element_type=F32)


def tn(left, right):
    return lax.dot_general(left, right, (((0,), (0,)), ((), ())), preferred_element_type=F32)


def gelu_pair(hidden):
    below = 0.5 * (1.0 + lax.erf(hidden * math.sqrt(0.5)))
    bell = jnp.exp(-0.5 * hidden * hidden)
    return hidden * below, below + hidden * bell * (1.0 / math.sqrt(2.0 * math.pi))


def unit(hidden):
    center = hidden - jnp.mean(hidden, axis=-1, keepdims=True)
    spread = jnp.mean(center * center, axis=-1, keepdims=True)
    rate = lax.rsqrt(spread + EPS)
    return center * rate, rate


def unit_back(normed, rate, grad, gain):
    scaled = grad * gain
    return rate * (
        scaled
        - jnp.mean(scaled, axis=-1, keepdims=True)
        - normed * jnp.mean(scaled * normed, axis=-1, keepdims=True)
    )


def lane_masks(head, lane):
    base = (head // 8) * 8
    return (lane // 64) == (head % 2), (lane // 16) == (head - base)


ORDERS = (((0, 2, 1, 3), (1, 0, 2, 3)), ((1, 2, 0, 3), (2, 0, 1, 3)), ((0, 2, 1, 3), (2, 0, 1, 3)), ((0, 1, 2, 3), (1, 0, 2, 3)))
FIELDS_DOWN = ((("down", 0, 192),),)
FIELDS_UP = ((("left", 0, 96), ("right", 0, 96), ("low", 0, 32)),)
FIELDS_HALF = (
    (("query", 0, 32), ("key", 0, 32), ("value", 0, 16), ("mix", 0, 16), ("low", 0, 16)),
    (("query", 256, 16), ("key", 256, 16), ("value", 128, 32), ("mix", 128, 32)),
)
PLANS = (FIELDS_DOWN, FIELDS_UP, FIELDS_HALF)
HALF_ROWS = {"query": 384, "key": 384, "value": 384, "mix": 384, "low": 128}
EVENTS = (
    "B2", "D.core", "B3", "U.core", "turn", "p0", "p1", "D0.0", "U0.0", "close", "in", "D0.1", "A.core",
    "U0.1", "D0.2", "U0.2", "A0.0", "A1.0", "D0.3", "A1.1", "A0.1", "U0.3", "A1.2", "A0.2", "U0.4", "D0.4",
    "A1.3", "A0.3", "A1.4", "A0.4", "A1.5", "U0.5", "D0.5", "A0.5", "D0.6", "oD", "A1.6", "A0.6", "U0.6",
    "oU",
)


def leaf_of(fields):
    return sum(n for _, _, n in fields)


def streams_of(plan):
    base = 0
    first = sum(len(p) for p in PLANS[:PLANS.index(plan)])
    for i, fields in enumerate(plan):
        yield first + i, base, leaf_of(fields), fields
        base += 8 * leaf_of(fields)


def rows_of(plan):
    return sum(8 * leaf_of(fields) for fields in plan)


def sides_of(dp, tensor):
    bits = [(dp >> b) & 1 for b in range(4)]
    values = [tensor & 1]
    for orders in ORDERS:
        values += [bits[o[0]] * 4 + bits[o[1]] * 2 + bits[o[2]] for o in orders]
    return jnp.stack(values)


def place(out, sides, core, plan, field, value, start=0, shift=0, skip=0):
    for number, base, leaf, fields in streams_of(plan):
        mask = sides[1 + 2 * number + core]
        inner = 0
        for name, first, n in fields:
            if name == field:
                for l in range(8):
                    at = first + l * n - start
                    if 0 <= at < value.shape[0]:
                        row = shift + base + inner + n * skip + leaf * jnp.bitwise_xor(mask, l)
                        row = pl.multiple_of(row, math.gcd(math.gcd(base + inner, leaf), 16))
                        out[pl.ds(row, n), :] = value[at:at + n, :]
            inner += n


def place_half(out, sides, field, value, skip=0):
    half = HALF_ROWS[field]
    for core in range(2):
        shift = jnp.bitwise_xor(sides[0], core) * rows_of(FIELDS_HALF)
        place(out, sides, core, FIELDS_HALF, field, value[core * half:(core + 1) * half, :], 0, shift, skip)


def fetch(pairs, sems):
    copies = [pltpu.make_async_copy(src, dst, sems.at[i]) for i, (src, dst) in enumerate(pairs)]
    for copy in copies:
        copy.start()
    return copies


def front_kernel(
    count_ref, sides, text_any, layout_any, joint_t_any, joint_l_any, mix_t_any, mix_l_any,
    qkv_t, qkv_l, mixed_t, mixed_l, normed_t, normed_l, stats,
    text_ref, layout_ref, joint_t, joint_l, mix_t, mix_l, mix_acc, flipped, sems,
):
    slots, width_t = text_ref.shape
    width_l = layout_ref.shape[1]
    columns = [slice(j * width_t, (j + 1) * width_t) for j in range(3)]
    copies = fetch(
        [
            (layout_any.at[0], flipped), (joint_l_any, joint_l), (text_any.at[0], text_ref),
            *((joint_t_any.at[:, c], joint_t.at[:, c]) for c in columns),
            (mix_t_any, mix_t), (mix_l_any, mix_l),
        ],
        sems,
    )
    count = count_ref[0]
    mix_acc[...] = jnp.zeros_like(mix_acc)
    stats[...] = jnp.zeros_like(stats)
    copies[0].wait()
    copies[1].wait()
    layout_ref[...] = flipped[...].T
    for j in range(3):
        qkv_l[:, j * 256:j * 256 + width_l] = nn(
            layout_ref[...], joint_l[:, j * width_l:(j + 1) * width_l]
        ).astype(BF16)
        qkv_l[:, j * 256 + width_l:(j + 1) * 256] = jnp.zeros((slots, 256 - width_l), BF16)
    copies[2].wait()

    def project(j, carry):
        c = pl.ds(pl.multiple_of(j * width_t, width_t), width_t)
        pltpu.make_async_copy(joint_t_any.at[:, c], joint_t.at[:, c], sems.at[3 + j]).wait()
        qkv_t[:, c] = nn(text_ref[...], joint_t[:, c]).astype(BF16)
        return carry

    lax.fori_loop(0, 3, project, 0)
    lane = lax.broadcasted_iota(jnp.int32, (slots, 128), 1)
    dead = lax.broadcasted_iota(jnp.int32, (slots, slots), 1) >= count

    def pair_step(pair, carry):
        spot = lambda start: pl.ds(pl.multiple_of(start, 128), 128)
        at_l = (pair // 4) * 128
        query_t, key_t, value_t = (qkv_t[:, spot(j * width_t + pair * 128)] for j in range(3))
        query_l, key_l, value_l = (qkv_l[:, spot(j * 256 + at_l)] for j in range(3))
        keys = jnp.concatenate([key_t, key_l], axis=1)
        values = jnp.concatenate([value_t, value_l], axis=1)
        masks = [lane_masks(2 * pair + side, lane) for side in range(2)]
        logits = []
        for mask_t, mask_l in masks:
            queries = jnp.concatenate(
                [
                    jnp.where(mask_t, query_t * 0.125, 0),
                    jnp.where(mask_l, query_l * 0.25, 0),
                ],
                axis=1,
            ).astype(BF16)
            logits.append(jnp.where(dead, NEG_FILL, nt(queries, keys)))
        outs = []
        for side in range(2):
            top = jnp.max(logits[side], axis=1, keepdims=True)
            raised = jnp.exp(logits[side] - top)
            mass = jnp.sum(raised, axis=1, keepdims=True)
            stats[...] = jnp.where(lane == 2 * pair + side, top + jnp.log(mass), stats[...])
            outs.append(nn(raised.astype(BF16), values) * (1.0 / mass))
        mixed_t[:, spot(pair * 128)] = jnp.where(masks[1][0], outs[1][:, :128], outs[0][:, :128]).astype(BF16)
        mix_acc[:, spot(at_l)] = (
            mix_acc[:, spot(at_l)]
            + jnp.where(masks[0][1], outs[0][:, 128:], 0.0)
            + jnp.where(masks[1][1], outs[1][:, 128:], 0.0)
        )
        return carry

    lax.fori_loop(0, HEADS // 2, pair_step, 0)
    mixed_l[...] = mix_acc[:, :width_l].astype(BF16)
    copies[6].wait()
    normed, rate = unit(text_ref[...].astype(F32) + nn(mixed_t[...], mix_t[...]))
    normed_t[...] = normed
    stats[...] = jnp.where(lane == 16, rate, stats[...])
    copies[7].wait()
    normed, rate = unit(layout_ref[...].astype(F32) + nn(mixed_l[...], mix_l[...]))
    normed_l[...] = normed
    stats[...] = jnp.where(lane == 17, rate, stats[...])


def column(stats, lane, which):
    return jnp.sum(jnp.where(lane == which, stats[...], 0.0), axis=1, keepdims=True)


ANY_SPEC = pl.BlockSpec(memory_space=pltpu.HBM)


def call(kernel, micros, outs, args, scratch=(), specs=None, aliases=None, limit=8, out_specs=None):
    moved = sum(math.prod(a.shape) * a.dtype.itemsize for a in args)
    return pl.pallas_call(
        kernel,
        out_shape=[(pltpu.VMEM(s, d) if kept else jax.ShapeDtypeStruct(s, d)) for s, d, kept in outs],
        in_specs=specs or [VMEM_SPEC] * len(args),
        out_specs=out_specs or [VMEM_SPEC] * len(outs),
        scratch_shapes=list(scratch),
        input_output_aliases=aliases or {},
        compiler_params=pltpu.CompilerParams(vmem_limit_bytes=limit * 1024 * 1024),
        cost_estimate=pl.CostEstimate(flops=int(micros * SCALE * 1.1e9), bytes_accessed=moved, transcendentals=0),
    )(*args)


def front(count, sides, text, layout, joint_t, joint_l, mix_t, mix_l):
    _, s, wt = text.shape
    wl = layout.shape[1]
    return call(
        front_kernel,
        12,
        [
            ((s, 3 * wt), BF16, True), ((s, 768), BF16, True), ((s, wt), BF16, True), ((s, wl), BF16, True),
            ((s, wt), F32, True), ((s, wl), F32, True), ((s, 128), F32, True),
        ],
        (count, sides, text, layout, joint_t, joint_l, mix_t, mix_l),
        [
            pltpu.VMEM((s, wt), BF16), pltpu.VMEM((s, wl), BF16), pltpu.VMEM((wt, 3 * wt), BF16),
            pltpu.VMEM((wl, 3 * wl), BF16), pltpu.VMEM((wt, wt), BF16), pltpu.VMEM((wl, wl), BF16),
            pltpu.VMEM((s, 256), F32), pltpu.VMEM((wl, s), BF16), pltpu.SemaphoreType.DMA((8,)),
        ],
        [SMEM_SPEC] * 2 + [ANY_SPEC] * 6,
        limit=48,
    )


def feed_kernel(
    sides, normed_t, normed_l, norms_t, norms_l, *refs,
):
    far_refs, refs = refs[:10], refs[10:]
    (
        result_t, result_l, second_t, second_l, dfeed_t, dfeed_l, low_t, low_l,
        act_t0, act_t1, slope_t0, slope_t1, act_l0, act_l1, slope_l0, slope_l1,
        dnorm_t, dnorm_l, down_far,
    ) = refs[:19]
    cot_t, cot_l, up_t0, up_t1, down_t0, down_t1, up_l0, up_l1, down_l0, down_l1 = far_refs
    step = 512
    cuts = [slice(at, at + step) for at in range(0, up_t0.shape[1], step)]
    first_t = normed_t[...] * norms_t[0:1, :] + norms_t[1:2, :]
    low_t[...] = first_t.astype(BF16)
    first_l = normed_l[...] * norms_l[0:1, :] + norms_l[1:2, :]
    low_l[...] = first_l.astype(BF16)
    for up, act, slope in ((up_t0, act_t0, slope_t0), (up_t1, act_t1, slope_t1)):
        for cut in cuts:
            active, rise = gelu_pair(nn(low_t[...], up[:, cut]))
            act[:, cut] = active.astype(BF16)
            slope[:, cut] = rise.astype(BF16)
    for up, act, slope in ((up_l0, act_l0, slope_l0), (up_l1, act_l1, slope_l1)):
        active, rise = gelu_pair(nn(low_l[...], up[...]))
        act[...] = active.astype(BF16)
        slope[...] = rise.astype(BF16)
    summed_l = first_l + nt(act_l0[...], down_l0[...]) + nt(act_l1[...], down_l1[...])
    summed_t = normed_t[...] * norms_t[0:1, :] + norms_t[1:2, :] + (
        nn(act_t0[...], down_t0[...]) + nn(act_t1[...], down_t1[...])
    )
    for summed, norms, cot, result, second, dfeed, dnorm in (
        (summed_t, norms_t, cot_t, result_t, second_t, dfeed_t, dnorm_t),
        (summed_l, norms_l, cot_l, result_l, second_l, dfeed_l, dnorm_l),
    ):
        normed, rate = unit(summed)
        value = (normed * norms[2:3, :] + norms[3:4, :]).astype(BF16)
        result[...] = value if result is result_t else value.T
        grad = (cot[0] if cot is cot_t else cot[0].T).astype(F32)
        dnorm[0:1, :] = jnp.sum(grad * normed, axis=0, keepdims=True)
        dnorm[1:2, :] = jnp.sum(grad, axis=0, keepdims=True)
        back = unit_back(normed, rate, grad, norms[2:3, :])
        second[...] = back
        dfeed[...] = back.astype(BF16)
    down_kernel(sides, 1, act_t1, dfeed_t, down_far)


def feed(sides, normed_t, normed_l, norms_t, norms_l, cot_t, cot_l, weights):
    s, wt = normed_t.shape
    wl = normed_l.shape[1]
    ht, hl = weights[0].shape[1], weights[4].shape[1]
    return call(
        feed_kernel,
        16,
        [((s, wt), BF16, False), ((wl, s), BF16, False)]
        + [((s, wt), F32, True), ((s, wl), F32, True)]
        + [((s, wt), BF16, True), ((s, wl), BF16, True)] * 2
        + [((s, ht), BF16, True)] * 4
        + [((s, hl), BF16, True)] * 4
        + [((2, wt), F32, True), ((2, wl), F32, True), ((ht, wt), BF16, False)],
        (sides, normed_t, normed_l, norms_t, norms_l, cot_t, cot_l) + tuple(weights),
        specs=[SMEM_SPEC] + [VMEM_SPEC] * 14,
        limit=13,
    )


def down_kernel(sides, far, act, dfeed, out):
    core = jnp.bitwise_xor(sides[0], far)
    (number, _, leaf, _), = streams_of(FIELDS_DOWN)
    mask = sides[1 + 2 * number + core]

    def chunk(c, carry):
        at = pl.ds(pl.multiple_of(c * 4 * leaf, 4 * leaf), 4 * leaf)
        value = tn(act[:, at], dfeed[...]).astype(BF16)
        for i in range(4):
            row = leaf * jnp.bitwise_xor(mask, 4 * c + i)
            out[pl.ds(pl.multiple_of(row, 16), leaf), :] = value[i * leaf:(i + 1) * leaf, :]
        return carry

    lax.fori_loop(0, 2, chunk, 0)


def up_body(
    sides, far, dfeed_t, dfeed_l, low_t, low_l, down_t, down_l, slope_t, slope_l, act_l, up_t, up_l, prev_t, prev_l,
    grads, dfirst_t, dfirst_l, dhid,
):
    wt = low_t.shape[1]
    wl = low_l.shape[1]
    core = jnp.bitwise_xor(sides[0], far)
    (number, _, leaf, fields), = streams_of(FIELDS_UP)
    mask = sides[1 + 2 * number + core]
    part = fields[0][2]

    def chunk(c, carry):
        at = pl.ds(pl.multiple_of(c * wt, wt), wt)
        dhid[:, at] = (nt(dfeed_t[...], down_t[at, :]) * slope_t[:, at].astype(F32)).astype(BF16)
        value = tn(low_t[...], dhid[:, at]).astype(BF16)
        for l in range(8):
            row = leaf * jnp.bitwise_xor(mask, l) + part * c
            grads[pl.ds(pl.multiple_of(row, 16), part), :] = value[l * part:(l + 1) * part, :]
        return carry

    lax.fori_loop(0, down_t.shape[0] // wt, chunk, 0)
    dfirst_t[...] = prev_t[...] + nt(dhid[...], up_t[...])
    hl = down_l.shape[1]
    dhidden = (nn(dfeed_l[...], down_l[...]) * slope_l[...].astype(F32)).astype(BF16)
    lower = tn(act_l[...], dfeed_l[...]).astype(BF16)
    packed = jnp.concatenate([tn(low_l[...], dhidden).astype(BF16), lower[:wl, :], lower[wl:, :]], axis=1)
    place(grads, sides, core, FIELDS_UP, "low", jnp.concatenate([packed, jnp.zeros((64, wt), BF16)], axis=0))
    dfirst_l[...] = prev_l[...] + nt(dhidden, up_l[...])


def up_kernel(sides, *refs):
    up_body(sides, 0, *refs)


def up_down_kernel(*refs):
    sides, act_t, refs = refs[0], refs[1], refs[2:]
    down_kernel(sides, 0, act_t, refs[0], refs[13])
    up_body(sides, 1, *refs[:13], *refs[14:])


def up_grad(sides, act_t, *args):
    dfeed_t, dfeed_l, low_t, low_l, down_t = args[:5]
    s, wt = low_t.shape
    wl = low_l.shape[1]
    ht = down_t.shape[0]
    outs = [((ht + wl + 64, wt), BF16, False), ((s, wt), F32, True), ((s, wl), F32, True)]
    scratch = [pltpu.VMEM((s, ht), BF16)]
    if act_t is None:
        specs = [SMEM_SPEC] + [VMEM_SPEC] * len(args)
        return call(up_kernel, 5, outs, (sides,) + args, scratch, specs)
    specs = [SMEM_SPEC] + [VMEM_SPEC] * (len(args) + 1)
    return call(up_down_kernel, 8, [((ht, wt), BF16, False)] + outs, (sides, act_t) + args, scratch, specs)


def turn_kernel(
    sides, mixed_t, mixed_l, normed_t, normed_l, stats, dfirst_t, dfirst_l, norms_t, norms_l, dnorm_t, dnorm_l, mix_t, mix_l,
    grads, dtext, dlayout, dmix_t, dmix_l, mix_low, norm_low, djoint_t, acc_l,
):
    slots, wt = mixed_t.shape
    wl = mixed_l.shape[1]
    acc_l[...] = jnp.zeros_like(acc_l)
    djoint_t[...] = jnp.zeros_like(djoint_t)
    lane = lax.broadcasted_iota(jnp.int32, (slots, 128), 1)
    kept = []
    for n, (first, normed, norms, dnorm, width, mixed, mix, dmix) in enumerate((
        (dfirst_t, normed_t, norms_t, dnorm_t, wt, mixed_t, mix_t, dmix_t),
        (dfirst_l, normed_l, norms_l, dnorm_l, wl, mixed_l, mix_l, dmix_l),
    )):
        grad = first[...]
        unitv = normed[...]
        gain_grad = jnp.sum(grad * unitv, axis=0, keepdims=True)
        shift_grad = jnp.sum(grad, axis=0, keepdims=True)
        rows = jnp.concatenate([gain_grad, shift_grad, dnorm[0:2, :]], axis=0)
        kept.append(jnp.concatenate(
            [rows.astype(BF16), jnp.zeros((12, width), BF16)], axis=0
        ) if width == wt else jnp.concatenate(
            [jnp.concatenate([rows.astype(BF16), jnp.zeros((4, wt - width), BF16)], axis=1), jnp.zeros((44, wt), BF16)],
            axis=0,
        ))
        resid = unit_back(unitv, column(stats, lane, 16 + n), grad, norms[0:1, :])
        low = resid.astype(BF16)
        if n == 0:
            dtext[...] = resid
            place_half(grads, sides, "mix", tn(mixed[...], low).astype(BF16))
            dmix[...] = nt(low, mix[...]).astype(BF16)
        else:
            dlayout[...] = resid
            mix_low[...] = tn(mixed[...], low).astype(BF16)
            dmix[:, :wl] = nt(low, mix[...]).astype(BF16)
            dmix[:, wl:] = jnp.zeros((slots, 256 - wl), BF16)
    norm_low[...] = jnp.concatenate(kept, axis=0)


def turn(*args):
    s, wt = args[1].shape
    wl = args[2].shape[1]
    rows = 4 * wt + wl + 64
    return call(
        turn_kernel,
        4,
        [
            ((rows, wt), BF16, True), ((s, wt), F32, True), ((s, wl), F32, True), ((s, wt), BF16, True),
            ((s, 256), BF16, True), ((wl, wl), BF16, True), ((64, wt), BF16, True), ((s, 3 * wt), BF16, True),
            ((s, 768), F32, True),
        ],
        args,
        specs=[SMEM_SPEC] + [VMEM_SPEC] * (len(args) - 1),
    )


def pairs_kernel(span_ref, count_ref, qkv_t, qkv_l, stats, dmix_t, dmix_l, djoint_in, acc_in, djoint_t, acc_l):
    slots, wt = dmix_t.shape
    count = count_ref[0]
    lane = lax.broadcasted_iota(jnp.int32, (slots, 128), 1)
    dead = lax.broadcasted_iota(jnp.int32, (slots, slots), 1) >= count

    def pair_step(pair, carry):
        spot = lambda start: pl.ds(pl.multiple_of(start, 128), 128)
        at_l = (pair // 4) * 128
        query_t, key_t, value_t = (qkv_t[:, spot(j * wt + pair * 128)] for j in range(3))
        query_l, key_l, value_l = (qkv_l[:, spot(j * 256 + at_l)] for j in range(3))
        upper_t = dmix_t[:, spot(pair * 128)]
        upper_l = dmix_l[:, spot(at_l)]
        keys = jnp.concatenate([key_t, key_l], axis=1)
        values = jnp.concatenate([value_t, value_l], axis=1)
        kept = None
        for side in range(2):
            head = 2 * pair + side
            mask_t, mask_l = lane_masks(head, lane)
            queries = jnp.concatenate(
                [
                    jnp.where(mask_t, query_t * 0.125, 0),
                    jnp.where(mask_l, query_l * 0.25, 0),
                ],
                axis=1,
            ).astype(BF16)
            logits = jnp.where(dead, NEG_FILL, nt(queries, keys))
            probs = jnp.exp(logits - column(stats, lane, head))
            own_t = jnp.where(mask_t, upper_t, 0).astype(BF16)
            own_l = jnp.where(mask_l, upper_l, 0).astype(BF16)
            grad_t = nt(own_t, value_t)
            grad_s = nt(jnp.concatenate([own_t, own_l], axis=1), values)
            score_t = (probs * (grad_t - jnp.sum(grad_t * probs, axis=1, keepdims=True))).astype(BF16)
            score_l = (probs * (grad_s - jnp.sum(grad_s * probs, axis=1, keepdims=True))).astype(BF16)
            dvalue = tn(probs.astype(BF16), jnp.concatenate([upper_t, upper_l], axis=1))
            dquery_t = nn(score_t, key_t) * 0.125
            dkey_t = tn(score_t, query_t) * 0.125
            dquery_l = nn(score_l, key_l) * 0.25
            dkey_l = tn(score_l, query_l) * 0.25
            if side == 0:
                kept = (dquery_t, dkey_t, dvalue[:, :128])
            else:
                for j, (old, new) in enumerate(zip(kept, (dquery_t, dkey_t, dvalue[:, :128]))):
                    djoint_t[:, spot(j * wt + pair * 128)] = jnp.where(mask_t, new, old).astype(BF16)
            for j, part in enumerate((dquery_l, dkey_l, dvalue[:, 128:])):
                at = spot(j * 256 + at_l)
                acc_l[:, at] = acc_l[:, at] + jnp.where(mask_l, part, 0.0)
        return carry

    lax.fori_loop(span_ref[0], span_ref[1], pair_step, 0)


def pairs(lo, hi, prev, *args):
    s, wt = args[4].shape
    span = jnp.array([lo, hi], jnp.int32)
    return call(
        pairs_kernel,
        3 * (hi - lo),
        [((s, 3 * wt), BF16, True), ((s, 768), F32, True)],
        (span,) + args + tuple(prev),
        specs=[SMEM_SPEC] * 2 + [VMEM_SPEC] * 7,
        aliases={7: 0, 8: 1},
    )


def close_kernel(
    sides, text_ref, layout_ref, djoint_t, acc_l, mix_low, norm_low, part_ref,
    grads, djoint_l,
):
    wt = text_ref.shape[2]
    wl = layout_ref.shape[1]
    def block(j, carry):
        value = tn(text_ref[0], djoint_t[:, pl.ds(pl.multiple_of(j * wt, wt), wt)]).astype(BF16)
        place_half(grads, sides, "query", value, j)
        return carry

    lax.fori_loop(0, 2, block, 0)
    place_half(grads, sides, "value", tn(text_ref[0], djoint_t[:, 2 * wt:]).astype(BF16))
    for j in range(3):
        djoint_l[:, j * wl:(j + 1) * wl] = acc_l[:, j * 256:j * 256 + wl].astype(BF16)
    low = jnp.concatenate([nn(layout_ref[0], djoint_l[...]).astype(BF16), mix_low[...]], axis=1)
    place_half(grads, sides, "low", jnp.concatenate([low, norm_low[...]], axis=0))


def close(*args):
    text, layout = args[1:3]
    _, s, wt = text.shape
    wl = layout.shape[1]
    return call(
        close_kernel,
        3,
        [(args[7].shape, BF16, True), ((s, 3 * wl), BF16, True)],
        args,
        specs=[SMEM_SPEC] + [VMEM_SPEC] * (len(args) - 1),
        aliases={7: 0},
    )


def inputs_kernel(djoint_t, djoint_l, joint_t, joint_l, dtext_in, dlayout_in, dtext, dlayout):
    dtext[...] = dtext_in[...] + nt(djoint_t[...], joint_t[...])
    dlayout[...] = (dlayout_in[...] + nt(djoint_l[...], joint_l[...])).T


def input_grads(*args):
    s, wt = args[4].shape
    wl = args[5].shape[1]
    return call(inputs_kernel, 3, [((s, wt), F32, False), ((wl, s), F32, False)], args)


AXES = ("dp", "tensor")


def swap(value, bits, many):
    dp, tensor = many
    pairs = []
    for d in range(dp):
        for t in range(tensor):
            to = (d, t ^ 1) if bits == -1 else (d ^ (1 << bits[t]), t)
            pairs.append((d * tensor + t, to[0] * tensor + to[1]))
    return lax.ppermute(value, AXES, pairs)


def cut_of(value, base, rows):
    return lax.slice_in_dim(value, base, base + rows, axis=0)


def tie(values, *others):
    got = lax.optimization_barrier((tuple(values), tuple(others)))
    return got[0]


class Stream:
    def __init__(self, fields, orders, many):
        self.half, self.orders, self.many = 4 * leaf_of(fields), orders, many

    def launch(self, phase, value):
        bits = tuple(order[min(phase, 6 - phase)] for order in self.orders)
        self.flying = swap(value, bits, self.many)
        return [value]

    def begin(self, own, got, base):
        half = self.half
        self.keep = cut_of(own, base, half) + cut_of(got, base, half)
        return self.launch(0, cut_of(own, base + half, half) + cut_of(got, base + half, half))

    def finish(self, phase, token):
        got, = tie([self.flying], *token)
        keep = self.keep
        if phase < 2:
            half = keep.shape[0] // 2
            self.keep = cut_of(keep, 0, half) + cut_of(got, 0, half)
            return self.launch(phase + 1, cut_of(keep, half, half) + cut_of(got, half, half))
        if phase == 6:
            self.keep = (keep, got)
            return [got]
        self.keep = keep + got if phase < 4 else jnp.concatenate([keep, got], axis=0)
        return self.launch(phase + 1, self.keep)


def unplace(parts, sides, core, plan, field, out, half=0, which=(0, 1)):
    runs = []
    for i, (number, _, leaf, fields) in enumerate(streams_of(plan)):
        mask = sides[1 + 2 * number + core]
        inner = 0
        for name, first, n in fields:
            if name == field:
                for side in which:
                    part = parts[2 * i + side]

                    def copy(r, carry, first=first, n=n, inner=inner, part=part, mask=mask, side=side, leaf=leaf):
                        row = core * half + first + n * jnp.bitwise_xor(mask, 4 * side + r)
                        source = pl.ds(pl.multiple_of(inner + r * leaf, 16), n)
                        out[pl.ds(pl.multiple_of(row, 16), n), :] = part[source, :].astype(F32)
                        return carry

                    lax.fori_loop(0, 4, copy, 0)
                    start = core * half + first + 4 * n * jnp.bitwise_xor(mask // 4, side)
                    runs.append(pl.ds(pl.multiple_of(start, 4 * n), 4 * n))
            inner += n
    return runs


def open_down_kernel(sides, *refs):
    parts, (out, buffer, sems) = refs[:-3], refs[-3:]
    unplace(parts, sides, sides[0], FIELDS_DOWN, "down", buffer)
    copy = pltpu.make_async_copy(buffer, out, sems.at[0])
    copy.start()
    copy.wait()


def open_up_kernel(sides, *refs):
    parts, (up_t, up_l, down_l, left, right, low, sems) = refs[:-7], refs[-7:]
    wt = up_t.shape[0]
    wl, hl = up_l.shape
    fill = functools.partial(unplace, parts, sides, sides[0], FIELDS_UP)
    flying = []
    for side in range(2):
        for field, columns, buffer in (("left", slice(0, wt), left), ("right", slice(wt, 2 * wt), right)):
            run, = fill(field, buffer, which=(side,))
            copy = pltpu.make_async_copy(buffer.at[run, :], up_t.at[run, columns], sems.at[len(flying)])
            copy.start()
            flying.append(copy)
    fill("low", low)
    up_l[...] = low[:wl, :hl]
    down_l[:, :wl] = low[:wl, hl:hl + wl].T
    down_l[:, wl:] = low[:wl, hl + wl:].T
    for copy in flying:
        copy.wait()


def send_half(own, other, sides, outs, which, sems):
    flying = []
    for field, out, columns, buffer in outs:
        for parts, core in ((own, sides[0]), (other, 1 - sides[0])):
            for run in unplace(parts, sides, core, FIELDS_HALF, field, buffer, HALF_ROWS[field], (which,)):
                copy = pltpu.make_async_copy(buffer.at[run, :], out.at[run, columns], sems.at[len(flying)])
                copy.start()
                flying.append(copy)
    return flying


def half_outs(joint_t, mix_t, buffers):
    wt = mix_t.shape[0]
    names = ("query", "key", "value", "mix")
    places = [(joint_t, slice(j * wt, (j + 1) * wt)) for j in range(3)] + [(mix_t, slice(0, wt))]
    return [(name, *there, buffer) for name, there, buffer in zip(names, places, buffers)]


def first_half_kernel(sides, *refs):
    count = len(FIELDS_HALF)
    spread = lambda refs: [ref for ref in refs for _ in range(2)]
    own, other = spread(refs[:count]), spread(refs[count:2 * count])
    joint_t, mix_t, mark, *buffers, sems = refs[2 * count:]
    mark[...] = jnp.zeros_like(mark)
    for copy in send_half(own, other, sides, half_outs(joint_t, mix_t, buffers), 0, sems):
        copy.wait()


def open_half_kernel(sides, *refs):
    count = 2 * len(FIELDS_HALF)
    own, other, refs = refs[:count], refs[count:2 * count], refs[2 * count + 2:]
    joint_t, mix_t, joint_l, mix_l, norm_t, norm_l, *buffers, low, sems = refs
    wl = mix_l.shape[0]
    flying = send_half(own, other, sides, half_outs(joint_t, mix_t, buffers), 1, sems)
    for parts, core in ((own, sides[0]), (other, 1 - sides[0])):
        unplace(parts, sides, core, FIELDS_HALF, "low", low, HALF_ROWS["low"])
    joint_l[...] = low[:wl, :3 * wl]
    mix_l[...] = low[:wl, 3 * wl:]
    norm_t[...] = low[wl:wl + 4, :]
    norm_l[...] = low[wl + 16:wl + 20, :wl]
    for copy in flying:
        copy.wait()


def open_half(sides, own_parts, to_far, wt, wl):
    buffers = [pltpu.VMEM((wt, wt), F32)] * 4
    sems = pltpu.SemaphoreType.DMA((4 * len(own_parts),))
    big = [((wt, 3 * wt), F32, False), ((wt, wt), F32, False)]
    keeps, gots = own_parts[0::2], own_parts[1::2]
    far_keeps = to_far(keeps, 0)
    *begun, mark = call(
        first_half_kernel, 3, big + [((8, 128), F32, False)], (sides, *keeps, *far_keeps), buffers + [sems],
        [SMEM_SPEC] + [VMEM_SPEC] * 2 * len(keeps), limit=24, out_specs=[ANY_SPEC] * 2 + [VMEM_SPEC],
    )
    gots = [tie([got], mark)[0] for got in gots]
    both = lambda one, two: [part for pair in zip(one, two) for part in pair]
    args = (sides, *both(keeps, gots), *both(far_keeps, to_far(gots, 1)), *begun)
    return call(
        open_half_kernel, 3,
        big + [(shape, F32, False) for shape in ((wl, 3 * wl), (wl, wl), (4, wt), (4, wl))],
        args, buffers + [pltpu.VMEM((256, wt), F32), sems],
        [SMEM_SPEC] + [VMEM_SPEC] * (len(args) - 3) + [ANY_SPEC] * 2,
        aliases={len(args) - 2: 0, len(args) - 1: 1}, limit=24,
        out_specs=[ANY_SPEC] * 2 + [VMEM_SPEC] * 4,
    )


def open_up(kernel, micros, direct, outs, buffers, sides, token, parts):
    if token:
        parts = [tie([parts[0]], *token)[0], *parts[1:]]
    return call(
        kernel, micros, [(shape, F32, False) for shape in outs], (sides,) + tuple(parts),
        [pltpu.VMEM(shape, F32) for shape in buffers] + [pltpu.SemaphoreType.DMA((4,))],
        [SMEM_SPEC] + [VMEM_SPEC] * len(parts), limit=24,
        out_specs=[ANY_SPEC] * direct + [VMEM_SPEC] * (len(outs) - direct),
    )


def shards(
    many, text_input, layout_input, page_counts, text_joint, text_mixing, text_norms, text_upward, text_downward,
    layout_joint, layout_mixing, layout_norms, layout_upward, layout_downward, text_cotangent, layout_cotangent,
):
    dp, tensor = many
    wt, wl = text_input.shape[2], layout_input.shape[2]
    layout_flip = layout_input.swapaxes(1, 2)
    halves = tensor == 2 and dp == 16
    own = (text_upward, text_downward, layout_upward, layout_downward.T)
    if halves:
        far = tuple(swap(w, -1, many) for w in own)
    else:
        whole = [
            lax.all_gather(w, "tensor", axis=axis, tiled=True) for w, axis in zip(own, (1, 0, 1, 1))
        ]
        cut = lambda w, axis, i: lax.slice_in_dim(w, i * (w.shape[axis] // 2), (i + 1) * (w.shape[axis] // 2), axis=axis)
        own = tuple(cut(w, axis, 0) for w, axis in zip(whole, (1, 0, 1, 1)))
        far = tuple(cut(w, axis, 1) for w, axis in zip(whole, (1, 0, 1, 1)))
    sides = sides_of(lax.axis_index("dp").astype(jnp.int32), lax.axis_index("tensor").astype(jnp.int32))
    if not halves:
        sides = jnp.zeros_like(sides)
    (
        qkv_t, qkv_l, mixed_t, mixed_l, normed_t, normed_l, stats,
    ) = front(page_counts, sides, text_input, layout_flip, text_joint, layout_joint, text_mixing, layout_mixing)
    up_t0, down_t0, up_l0, down_l0 = own
    up_t1, down_t1, up_l1, down_l1 = far
    (
        result_t, result_l, second_t, second_l, dfeed_t, dfeed_l, low_t, low_l,
        act_t0, act_t1, slope_t0, slope_t1, act_l0, act_l1, slope_l0, slope_l1, dnorm_t, dnorm_l, down_far,
    ) = feed(
        sides, normed_t, normed_l, text_norms, layout_norms, text_cotangent, layout_cotangent.swapaxes(1, 2),
        (own[0], far[0], own[1], far[1], own[2], far[2], own[3], far[3]),
    )
    run = {"token": [dfeed_t], "state": None, "first": (second_t, second_l)}
    streams = {
        "%s%d" % (name, number - first): Stream(fields, ORDERS[number], many)
        for name, plan in zip("DUA", PLANS)
        for first in [sum(len(p) for p in PLANS[:PLANS.index(plan)])]
        for number, _, _, fields in streams_of(plan)
    }
    got = {}
    if halves:
        got["D"] = swap(down_far, -1, many)

    def held(value):
        return tie([value], *run["token"])[0]

    def far_grads():
        down_own, up_far, *run["first"] = up_grad(
            sides, act_t0, held(dfeed_t),
            dfeed_l, low_t, low_l, down_t1, down_l1, slope_t1, slope_l1, act_l1, up_t1, up_l1, *run["first"]
        )
        run["down_own"], run["up_far"], run["token"] = down_own, up_far, [run["first"][0]]
        if halves:
            got["U"] = swap(up_far, -1, many)

    def own_grads():
        run["up_own"], *run["first"] = up_grad(
            sides, None, held(dfeed_t),
            dfeed_l, low_t, low_l, down_t0, down_l0, slope_t0, slope_l0, act_l0, up_t0, up_l0, *run["first"]
        )
        run["token"] = [run["first"][0]]

    def turn_back():
        run["grads"], run["dtext"], run["dlayout"], run["dmix_t"], run["dmix_l"], run["mix_low"], run["norm_low"], *run["state"] = turn(
            sides, mixed_t, mixed_l, normed_t, normed_l, stats, held(run["first"][0]), run["first"][1], text_norms,
            layout_norms, dnorm_t, dnorm_l, text_mixing, layout_mixing,
        )
        run["token"] = [run["dmix_t"]]

    def pair_grads(lo, hi):
        run["state"] = pairs(
            lo, hi, run["state"], page_counts, qkv_t, qkv_l, stats, held(run["dmix_t"]), run["dmix_l"]
        )
        run["token"] = [run["state"][1]]

    def close_up():
        state = run["state"]
        run["grads"], run["djoint_l"] = close(
            sides, text_input, layout_flip, state[0], held(state[1]), run["mix_low"], run["norm_low"], run["grads"],
        )
        run["token"] = [run["djoint_l"]]
        if halves:
            rows = run["grads"].shape[0] // 2
            run["half_own"] = cut_of(run["grads"], 0, rows)
            got["A"] = swap(cut_of(run["grads"], rows, rows), -1, many)

    def inputs_up():
        run["dtext"], run["dlayout"] = input_grads(
            run["state"][0], held(run["djoint_l"]), text_joint, layout_joint, run["dtext"], run["dlayout"]
        )
        run["token"] = [run["dlayout"]]

    ht, hl = text_upward.shape[1], layout_upward.shape[1]

    def parts_of(name, plan):
        return [part for i in range(len(plan)) for part in streams["%s%d" % (name, i)].keep]

    def open_down():
        run["down"], = open_up(open_down_kernel, 3, 1, [(ht, wt)], [(ht, wt)], sides, run["token"], parts_of("D", FIELDS_DOWN))
        run["token"] = [run["down"]]

    def open_upper():
        run["up"] = open_up(
            open_up_kernel, 3, 1, [(wt, ht), (wl, hl), (wl, hl)], [(wt, wt)] * 2 + [(256, wt)], sides, run["token"], parts_of("U", FIELDS_UP)
        )
        run["token"] = [run["up"][1]]

    kernels = {
        "B2": far_grads, "B3": own_grads, "turn": turn_back, "p0": lambda: pair_grads(0, 3),
        "p1": lambda: pair_grads(3, 6), "close": close_up, "in": inputs_up,
    }
    opens = {"oD": open_down, "oU": open_upper}
    owns = {"D": ("down_own", FIELDS_DOWN), "U": ("up_own", FIELDS_UP), "A": ("half_own", FIELDS_HALF)}
    for event in EVENTS if halves else [e for e in EVENTS if e in kernels]:
        if event in kernels:
            kernels[event]()
        elif event in opens:
            opens[event]()
        else:
            name, step = event.split(".")
            if step == "core":
                here, = tie([got[name]], *run["token"])
                own_of, plan = owns[name]
                run["token"], base = [], 0
                for i, fields in enumerate(plan):
                    run["token"] += streams["%s%d" % (name, i)].begin(run[own_of], here, base)
                    base += 8 * leaf_of(fields)
            else:
                run["token"] = streams[name].finish(int(step), run["token"])
    grads, dtext, dlayout = run["grads"], run["dtext"], run["dlayout"]
    down_own, up_own, up_far = run["down_own"], run["up_own"], run["up_far"]

    if halves:
        own_parts = parts_of("A", FIELDS_HALF)
        down_grad_t = run["down"]
        up_grad_t, up_grad_l, down_grad_l = run["up"]
        down_grad_l = down_grad_l.T
        joint_t, mix_t, joint_l, mix_l, norm_t, norm_l = open_half(
            sides, own_parts, lambda parts, side: [swap(part, -1, many) for part in parts], wt, wl
        )
    else:
        def parts(packed, plan, shift=0):
            return [
                cut_of(packed, shift + base + i * 4 * leaf, 4 * leaf)
                for _, base, leaf, _ in streams_of(plan) for i in range(2)
            ]

        hidden, wide = down_own.shape[0], up_l0.shape[1]
        downs = [
            open_up(open_down_kernel, 3, 1, [(hidden, wt)], [(hidden, wt)], sides, [], parts(p, FIELDS_DOWN))[0]
            for p in (down_own, down_far)
        ]
        ups = [
            open_up(
                open_up_kernel, 3, 1, [(wt, hidden), (wl, wide), (wl, wide)], [(wt, wt)] * 2 + [(256, wt)], sides, [],
                parts(p, FIELDS_UP),
            )
            for p in (up_own, up_far)
        ]
        joined = [
            jnp.concatenate([ups[0][0], ups[1][0]], axis=1),
            jnp.concatenate(downs, axis=0),
            jnp.concatenate([ups[0][1], ups[1][1]], axis=1),
            jnp.concatenate([ups[0][2].T, ups[1][2].T], axis=0),
        ]
        up_grad_t, down_grad_t, up_grad_l, down_grad_l = (
            lax.psum(lax.psum_scatter(g, "tensor", scatter_dimension=axis, tiled=True), "dp")
            for g, axis in zip(joined, (1, 0, 1, 0))
        )
        rows = grads.shape[0] // 2
        far_parts = parts(grads, FIELDS_HALF, rows)
        joint_t, mix_t, joint_l, mix_l, norm_t, norm_l = lax.psum(
            open_half(sides, parts(grads, FIELDS_HALF), lambda parts, side: far_parts[side::2], wt, wl), AXES
        )
    return (
        result_t[None],
        result_l.T[None],
        dtext[None],
        dlayout.T[None],
        joint_t,
        mix_t,
        norm_t,
        up_grad_t.astype(F32),
        down_grad_t.astype(F32),
        joint_l,
        mix_l,
        norm_l,
        up_grad_l.astype(F32),
        down_grad_l.astype(F32),
    )


def solution(mesh):
    many = (mesh.shape["dp"], mesh.shape["tensor"])
    pages = P(("dp", "tensor"), None, None)
    columns, rows = P(None, "tensor"), P("tensor", None)
    return jax.shard_map(
        functools.partial(shards, many),
        mesh=mesh,
        in_specs=(
            pages, pages, P(("dp", "tensor")), P(), P(), P(), columns, rows, P(), P(), P(), columns, rows, pages, pages,
        ),
        out_specs=(
            pages, pages, pages, pages, P(), P(), P(), columns, rows, P(), P(), P(), columns, rows,
        ),
        check_vma=False,
    )
```
